32 devices in a mesh: wide: 8 (over z, y), narrow: 4 (over x, core).
Axes of the slice: x: 2, y: 2, z: 4, core: 2. Of those that a mesh axis runs over, the one named last changes fastest.
Arguments:
- patches: bfloat16 [128, 256, 768], P(('wide', 'narrow')), may hold values from -6 to 6
- counts: int32 [128], P(('wide', 'narrow')), may hold values from 16 to 256, as said below
- cotangent: bfloat16 [128, 256, 768], P(('wide', 'narrow')), may hold values from -6 to 6
- input_weight: bfloat16 [768, 2304], P(('wide', 'narrow')), may hold values from -0.21875 to 0.21875
- output_weight: bfloat16 [768, 768], P(('wide', 'narrow')), may hold values from -0.875 to 0.875
- expand_weight: bfloat16 [768, 3072], P(('wide', 'narrow')), may hold values from -0.21875 to 0.21875
- reduce_weight: bfloat16 [3072, 768], P(('wide', 'narrow')), may hold values from -0.15625 to 0.15625
- norm1_gain: bfloat16 [768], P(('wide', 'narrow')), may hold values from 0.5 to 1.5
- norm1_shift: bfloat16 [768], P(('wide', 'narrow')), may hold values from -1.75 to 1.75
- query_bias: bfloat16 [768], P(('wide', 'narrow')), may hold values from -3 to 3
- value_bias: bfloat16 [768], P(('wide', 'narrow')), may hold values from -1.75 to 1.75
- output_bias: bfloat16 [768], P(('wide', 'narrow')), may hold values from -1.75 to 1.75
- branch1_scale: bfloat16 [768], P(('wide', 'narrow')), may hold values from 0.29882812 to 1.5
- norm2_gain: bfloat16 [768], P(('wide', 'narrow')), may hold values from 0.5 to 1.5
- norm2_shift: bfloat16 [768], P(('wide', 'narrow')), may hold values from -1.75 to 1.75
- expand_bias: bfloat16 [3072], P(('wide', 'narrow')), may hold values from -3 to 3
- reduce_bias: bfloat16 [768], P(('wide', 'narrow')), may hold values from -1.75 to 1.75
- branch2_scale: bfloat16 [768], P(('wide', 'narrow')), may hold values from 0.29882812 to 1.5
Outputs:
- activations: bfloat16 [128, 256, 768], P(('wide', 'narrow'))
- input_grad: float32 [128, 256, 768], P(('wide', 'narrow'))
- input_weight_grad: float32 [768, 2304], P(('wide', 'narrow'))
- output_weight_grad: float32 [768, 768], P(('wide', 'narrow'))
- expand_weight_grad: float32 [768, 3072], P(('wide', 'narrow'))
- reduce_weight_grad: float32 [3072, 768], P(('wide', 'narrow'))
- norm1_gain_grad: float32 [768], P(('wide', 'narrow'))
- norm1_shift_grad: float32 [768], P(('wide', 'narrow'))
- query_bias_grad: float32 [768], P(('wide', 'narrow'))
- value_bias_grad: float32 [768], P(('wide', 'narrow'))
- output_bias_grad: float32 [768], P(('wide', 'narrow'))
- branch1_scale_grad: float32 [768], P(('wide', 'narrow'))
- norm2_gain_grad: float32 [768], P(('wide', 'narrow'))
- norm2_shift_grad: float32 [768], P(('wide', 'narrow'))
- expand_bias_grad: float32 [3072], P(('wide', 'narrow'))
- reduce_bias_grad: float32 [768], P(('wide', 'narrow'))
- branch2_scale_grad: float32 [768], P(('wide', 'narrow'))
The draws below stay inside these ranges and needn't reach their ends.
Inputs may be any that keep to these rules, and one draw needn't show every extreme that they name: `counts`: valid patches of each image, heavy-tailed; every draw holds full images and images with only 16 valid patches.
All inputs are finite; a program needn't handle non-finite values.
Results may differ from the reference program's by a relative error of at most 0.015.
Values may be sent and summed in bfloat16 or wider, within the bound.
No kernel may reach another device: no remote copies, remote signals or barrier semaphores. Data moves between devices by JAX's collectives and lax.ppermute only.
A program may use at most 192 MiB of HBM per device.

```python
import math
import jax
import jax.numpy as jnp
from jax import lax

D = 768
HEADS = 12
HEAD = 64
FF = 3072
PATCHES = 256
IMAGES = 128


def draw_counts(key, part):
    scale_key = jax.random.fold_in(key, 11)
    extra_key = jax.random.fold_in(key, 12)
    powers = jax.random.randint(scale_key, (IMAGES,), 0, 5)
    lowest = PATCHES // 16 * jnp.left_shift(jnp.ones((IMAGES,), jnp.int32), powers)
    extra = jax.random.randint(extra_key, (IMAGES,), 0, lowest)
    counts = jnp.minimum(PATCHES, lowest + extra).astype(jnp.int32)
    counts = counts.at[0].set(PATCHES)
    counts = counts.at[1].set(PATCHES // 16)
    return counts


def levels(rng, dims, shards, least, high):
    def one(dim, blocks):
        heights = jax.random.uniform(jax.random.fold_in(jax.random.fold_in(rng, 6), dim), (blocks,), jnp.float32, least / len(shards), high / len(shards))
        return jnp.repeat(jnp.exp(heights), dims[dim] // blocks).reshape((-1,) + (1,) * (len(dims) - dim - 1))

    gain = one(*shards[0])
    for cut in shards[1:]:
        gain = gain * one(*cut)
    return gain


def normal_values(own_key, dims, scale, limit, cuts=(), held_as=jnp.bfloat16):
    level = levels(own_key, dims, cuts, -0.22, 0.18) if cuts else 1.0
    array = jax.random.normal(own_key, dims, jnp.float32) * scale * level
    return jnp.minimum(jnp.maximum(array, -limit), limit).astype(held_as)


def setup_inputs(seed: int = 0) -> dict:
    key_list = jax.random.split(jax.random.key(seed), 19)
    return {
        "patches": normal_values(key_list[0], (IMAGES, PATCHES, D), 1.0, 6.0, ((0, 32),)),
        "counts": draw_counts(jax.random.fold_in(key_list[18], 71), 0),
        "cotangent": normal_values(key_list[2], (IMAGES, PATCHES, D), 1.0, 6.0, ((0, 32),)),
        "input_weight": normal_values(key_list[3], (D, 3 * D), D ** -0.5, 0.21875, ((0, 32),)),
        "output_weight": normal_values(key_list[4], (D, D), (D // 16) ** -0.5, 0.875, ((0, 32),)),
        "expand_weight": normal_values(key_list[5], (D, FF), D ** -0.5, 0.21875, ((0, 32),)),
        "reduce_weight": normal_values(key_list[6], (FF, D), (FF // 2) ** -0.5, 0.15625, ((0, 32),)),
        "norm1_gain": jnp.clip(1.0 + 0.1 * jax.random.normal(key_list[7], (D,), jnp.float32), 0.5, 1.5).astype(jnp.bfloat16),
        "norm1_shift": normal_values(key_list[8], (D,), 0.3, 1.75, ((0, 32),)),
        "query_bias": normal_values(key_list[9], (D,), 0.5, 3.0, ((0, 32),)),
        "value_bias": normal_values(key_list[10], (D,), 0.3, 1.75, ((0, 32),)),
        "output_bias": normal_values(key_list[11], (D,), 0.3, 1.75, ((0, 32),)),
        "branch1_scale": jnp.clip(jnp.exp(math.log(1.5) - 1.6133518 * jax.random.uniform(key_list[12], (D,), jnp.float32) ** levels(key_list[12], (D,), ((0, 32),), -0.2, 0.2)), 0.29882812, 1.5).astype(jnp.bfloat16),
        "norm2_gain": jnp.clip(1.0 + 0.1 * jax.random.normal(key_list[13], (D,), jnp.float32), 0.5, 1.5).astype(jnp.bfloat16),
        "norm2_shift": normal_values(key_list[14], (D,), 0.3, 1.75, ((0, 32),)),
        "expand_bias": normal_values(key_list[15], (FF,), 0.5, 3.0, ((0, 32),)),
        "reduce_bias": normal_values(key_list[16], (D,), 0.3, 1.75, ((0, 32),)),
        "branch2_scale": jnp.clip(jnp.exp(math.log(1.5) - 1.6133518 * jax.random.uniform(key_list[17], (D,), jnp.float32) ** levels(key_list[17], (D,), ((0, 32),), -0.2, 0.2)), 0.29882812, 1.5).astype(jnp.bfloat16),
    }


@jax.custom_vjp
def low(v):
    return lax.optimization_barrier(v.astype(jnp.bfloat16)).astype(jnp.float32)

@jax.custom_vjp
def low_back(v):
    return v

def low_keep(v):
    return (low(v), None)

def low_pass(kept, grad):
    return (grad,)

def back_keep(v):
    return (v, None)

def back_low(kept, grad):
    return (low(grad),)
low.defvjp(low_keep, low_pass)
low_back.defvjp(back_keep, back_low)

def layer_norm(inputs, norm_gain, norm_shift):
    average = lax.optimization_barrier(jnp.mean(inputs, axis=-1, keepdims=True))
    centered = inputs - average
    spread = lax.optimization_barrier(jnp.mean(centered * centered, axis=-1, keepdims=True))
    return centered * lax.rsqrt(spread + 1e-06) * norm_gain + norm_shift

def matmul(left, right):
    return jnp.dot(left, right, preferred_element_type=jnp.float32, precision=lax.Precision.HIGHEST)

def forward(block_in, valid_keys, params):
    input_weight, output_weight, expand_weight, reduce_weight, norm1_gain, norm1_shift, query_bias, value_bias, output_bias, branch1_scale, norm2_gain, norm2_shift, expand_bias, reduce_bias, branch2_scale = params
    group_size = block_in.shape[0]
    row_count = group_size * PATCHES
    head_shape = (group_size, PATCHES, HEADS, HEAD)
    flat_rows = block_in.reshape(row_count, D)
    normed = low(layer_norm(flat_rows, norm1_gain, norm1_shift))
    projections = matmul(normed, input_weight)
    queries = low(low_back(projections[:, :D] + query_bias)).reshape(head_shape)
    key_rows = low(low_back(projections[:, D:2 * D])).reshape(head_shape)
    values = low(low_back(projections[:, 2 * D:] + value_bias)).reshape(head_shape)
    raw_scores = jnp.einsum('gphd,gqhd->ghpq', queries, key_rows, precision=lax.Precision.HIGHEST) * HEAD ** (-0.5)
    scores = low_back(raw_scores)
    scores = jnp.where(valid_keys[:, None, None, :], scores, -1e+30)
    log_total = jax.nn.logsumexp(scores, axis=-1, keepdims=True)
    soft_weights = low(jnp.exp(scores - log_total))
    attended = jnp.einsum('ghpq,gqhd->gphd', soft_weights, values, precision=lax.Precision.HIGHEST)
    attended = low(low_back(attended.reshape(row_count, D)))
    projected = low_back(matmul(attended, output_weight) + output_bias)
    middle = flat_rows + branch1_scale * projected
    second = low(layer_norm(middle, norm2_gain, norm2_shift))
    hidden = low_back(matmul(second, expand_weight) + expand_bias)
    activated = low(jax.nn.gelu(hidden, approximate=False))
    branch = low_back(matmul(activated, reduce_weight) + reduce_bias)
    return (middle + branch2_scale * branch).reshape(group_size, PATCHES, D)

def reference(patches, counts, cotangent, input_weight, output_weight, expand_weight, reduce_weight, norm1_gain, norm1_shift, query_bias, value_bias, output_bias, branch1_scale, norm2_gain, norm2_shift, expand_bias, reduce_bias, branch2_scale):
    params = tuple((item.astype(jnp.float32) for item in (input_weight, output_weight, expand_weight, reduce_weight, norm1_gain, norm1_shift, query_bias, value_bias, output_bias, branch1_scale, norm2_gain, norm2_shift, expand_bias, reduce_bias, branch2_scale)))
    images = patches.shape[0]
    blocks = images // 16
    position = jnp.arange(PATCHES, dtype=jnp.int32)
    valid = position[None, :] < counts[:, None].astype(jnp.int32)
    row_mask = jnp.where(valid, 1.0, 0.0).astype(jnp.float32)
    inputs = patches.astype(jnp.float32).reshape(blocks, 16, PATCHES, D)
    cotans = (cotangent.astype(jnp.float32) * row_mask[:, :, None]).reshape(blocks, 16, PATCHES, D)
    valid_blocks = valid.reshape(blocks, 16, PATCHES)

    def one_step(totals, pieces):
        block_in, block_valid, block_cot = pieces

        def local_forward(inner_in, inner_params):
            return forward(inner_in, block_valid, inner_params)
        result, backward = jax.vjp(local_forward, block_in, params)
        grad_in, grad_params = backward(block_cot)
        return (jax.tree.map(jnp.add, totals, grad_params), (result.astype(jnp.bfloat16), grad_in))
    zeros = jax.tree.map(jnp.zeros_like, params)
    totals, (results, grads_in) = lax.scan(one_step, zeros, (inputs, valid_blocks, cotans))
    return (results.reshape(images, PATCHES, D), grads_in.reshape(images, PATCHES, D), totals[0], totals[1], totals[2], totals[3], totals[4], totals[5], totals[6], totals[7], totals[8], totals[9], totals[10], totals[11], totals[12], totals[13], totals[14])
```

```python
from functools import partial

import jax
import jax.numpy as jnp
from jax import lax
from jax.sharding import PartitionSpec as P

HEADS = 12
HEAD = 64
AXES = ("wide", "narrow")
LANES = 128


def shuffle(value, count, target):
    return lax.ppermute(value, AXES, [(d, target(d)) for d in range(count)])

def digits(planes):
    radices = []
    while planes > 1:
        radix = 4 if planes % 4 == 0 else 2 if planes % 2 == 0 else planes
        radices.append(radix)
        planes //= radix
    return radices


def shifted(device, stride, radix, step):
    digit = (device // stride) % radix
    return device + (((digit + step) % radix) - digit) * stride


def gather_z(shard, count):
    me = lax.axis_index(AXES)
    held = shard[None]
    stride = 8
    for radix in digits(count // 8):
        mine = (me // stride) % radix
        out = jnp.zeros((radix,) + held.shape, held.dtype)
        pieces = [held] + [
            shuffle(held, count, lambda d, s=s: shifted(d, stride, radix, s))
            for s in range(1, radix)
        ]
        for s, piece in enumerate(pieces):
            out = lax.dynamic_update_index_in_dim(out, piece, (mine - s) % radix, 0)
        held = out.reshape((-1,) + shard.shape)
        stride *= radix
    return held


def gather_xy(plane, count):
    planes = plane.shape[0]
    half = planes // 2
    across_x = shuffle(plane, count, lambda d: d ^ 2)
    across_y = shuffle(plane, count, lambda d: d ^ 4)
    far_a = shuffle(across_y[:half], count, lambda d: d ^ 2)
    far_b = shuffle(across_x[half:], count, lambda d: d ^ 4)
    return plane, across_x, across_y, far_a, far_b

def assemble(pieces, count):
    plane, across_x, across_y, far_a, far_b = pieces
    planes, rows, cols = plane.shape
    half = planes // 2
    me = lax.axis_index(AXES)
    core = me % 2
    spot = (me // 2) % 4
    held = jnp.zeros((planes, 4, rows, cols), plane.dtype)
    def put(buf, item, z, yx):
        return lax.dynamic_update_slice(buf, item[:, None], (z, yx, 0, 0))
    held = put(held, plane, 0, spot)
    held = put(held, across_x, 0, spot ^ 1)
    held = put(held, across_y, 0, spot ^ 2)
    held = put(held, far_a, 0, spot ^ 3)
    held = put(held, far_b, half, spot ^ 3)
    other = shuffle(held, count, lambda d: d ^ 1)
    full = jnp.zeros((planes, 4, 2, rows, cols), plane.dtype)
    full = lax.dynamic_update_slice(full, held[:, :, None], (0, 0, core, 0, 0))
    full = lax.dynamic_update_slice(full, other[:, :, None], (0, 0, 1 - core, 0, 0))
    return full.reshape(count * rows, cols)

def gather(shard, count):
    return assemble(gather_xy(gather_z(shard, count), count), count)

def take(value, index, axis):
    return lax.dynamic_index_in_dim(value, index, axis, keepdims=False)

def scatter_core(parts, count):
    me = lax.axis_index(AXES)
    core = me % 2
    planes = count // 8
    split = [p.reshape(planes, 4, 2, p.shape[0] // count, p.shape[1]) for p in parts]
    send = jnp.concatenate([take(p, 1 - core, 2) for p in split], axis=-1)
    keep = jnp.concatenate([take(p, core, 2) for p in split], axis=-1)
    got = shuffle(send, count, lambda d: d ^ 1)
    return (keep.astype(jnp.float32) + got.astype(jnp.float32)).astype(jnp.bfloat16)

def scatter_xy(held, count):
    planes = held.shape[0]
    half = planes // 2
    spot = (lax.axis_index(AXES) // 2) % 4
    f = jnp.float32
    far = take(held, spot ^ 3, 1)
    got_a = shuffle(far[:half], count, lambda d: d ^ 2)
    got_b = shuffle(far[half:], count, lambda d: d ^ 4)
    to_y = take(held, spot ^ 2, 1)
    to_y = jnp.concatenate([(to_y[:half].astype(f) + got_a.astype(f)).astype(jnp.bfloat16), to_y[half:]], axis=0)
    to_x = take(held, spot ^ 1, 1)
    to_x = jnp.concatenate([to_x[:half], (to_x[half:].astype(f) + got_b.astype(f)).astype(jnp.bfloat16)], axis=0)
    from_x = shuffle(to_x, count, lambda d: d ^ 2)
    from_y = shuffle(to_y, count, lambda d: d ^ 4)
    mine = take(held, spot, 1)
    return mine.astype(f) + from_x.astype(f) + from_y.astype(f)

def scatter_z(column, count):
    me = lax.axis_index(AXES)
    total = column
    stride = count
    for radix in digits(count // 8)[::-1]:
        stride //= radix
        mine = (me // stride) % radix
        split = total.reshape((radix, -1) + column.shape[1:])
        low = split.astype(jnp.bfloat16)
        total = take(split, mine, 0)
        for s in range(1, radix):
            item = take(low, (mine + s) % radix, 0)
            came = shuffle(item, count, lambda d, s=s: shifted(d, stride, radix, s))
            total = total + came.astype(jnp.float32)
    return total[0]


def scatter(parts, count):
    return scatter_z(scatter_xy(scatter_core(parts, count), count), count)


def layer_norm(inputs, norm_gain, norm_shift):
    average = jnp.mean(inputs, axis=-1, keepdims=True)
    centered = inputs - average
    spread = jnp.mean(centered * centered, axis=-1, keepdims=True)
    return centered * lax.rsqrt(spread + 1e-06) * norm_gain + norm_shift


def contract_rows(left, right):
    return lax.dot_general(
        left, right, (((0,), (0,)), ((), ())), preferred_element_type=jnp.float32
    )


def contract_cols(left, right):
    return lax.dot_general(
        left, right, (((1,), (1,)), ((), ())), preferred_element_type=jnp.float32
    )


def column_sum(values):
    return jnp.sum(values.astype(jnp.float32), axis=0)


def per_device(
    patches,
    counts,
    cotangent,
    input_weight,
    output_weight,
    expand_weight,
    reduce_weight,
    norm1_gain,
    norm1_shift,
    query_bias,
    value_bias,
    output_bias,
    branch1_scale,
    norm2_gain,
    norm2_shift,
    expand_bias,
    reduce_bias,
    branch2_scale,
):
    count = lax.axis_size("wide") * lax.axis_size("narrow")
    vectors = (
        norm1_gain,
        norm1_shift,
        query_bias,
        value_bias,
        output_bias,
        branch1_scale,
        norm2_gain,
        norm2_shift,
        reduce_bias,
        branch2_scale,
    )
    shard_rows = input_weight.shape[0]
    fold = expand_bias.shape[0] // shard_rows
    side = jnp.concatenate(
        [jnp.stack(vectors, axis=1), expand_bias.reshape(shard_rows, fold)], axis=1
    )
    side = jnp.pad(side, ((0, 0), (0, LANES - side.shape[1])))
    first = gather(jnp.concatenate([input_weight, side], axis=1), count)
    second = gather(jnp.concatenate([output_weight, expand_weight], axis=1), count)
    w_reduce = gather(reduce_weight, count)
    columns = input_weight.shape[1]
    w_input = first[:, :columns]
    w_output = second[:, : output_weight.shape[1]]
    w_expand = second[:, output_weight.shape[1] :]
    side_all = first[:, columns:].astype(jnp.float32)
    (
        gain_one,
        shift_one,
        bias_query,
        bias_value,
        bias_output,
        scale_one,
        gain_two,
        shift_two,
        bias_reduce,
        scale_two,
    ) = tuple(side_all[:, t] for t in range(len(vectors)))
    bias_expand = side_all[:, len(vectors) : len(vectors) + fold].reshape(-1)
    n_images, n_patch, width = patches.shape
    n_rows = n_images * n_patch
    head_shape = (n_images, n_patch, HEADS, HEAD)
    score_scale = HEAD ** (-0.5)
    position = jnp.arange(n_patch, dtype=jnp.int32)
    valid_keys = position[None, :] < counts[:, None]
    row_mask = jnp.where(valid_keys, 1.0, 0.0).astype(jnp.float32).reshape(n_rows, 1)
    rows_in = patches.astype(jnp.float32).reshape(n_rows, width)
    normed_low = layer_norm(rows_in, gain_one, shift_one).astype(jnp.bfloat16)
    projections = jnp.dot(normed_low, w_input, preferred_element_type=jnp.float32)
    queries = (projections[:, :width] + bias_query).astype(jnp.bfloat16).reshape(head_shape)
    key_rows = projections[:, width : 2 * width].astype(jnp.bfloat16).reshape(head_shape)
    values = (projections[:, 2 * width :] + bias_value).astype(jnp.bfloat16).reshape(head_shape)

    def attention_scores():
        raw_scores = jnp.einsum(
            "iphd,iqhd->ihpq", queries, key_rows, preferred_element_type=jnp.float32
        )
        return jnp.where(valid_keys[:, None, None, :], raw_scores * score_scale, -1e30)

    scores = attention_scores()
    log_total = jax.nn.logsumexp(scores, axis=-1, keepdims=True)
    soft_low = jnp.exp(scores - log_total).astype(jnp.bfloat16)
    attended = jnp.einsum("ihpq,iqhd->iphd", soft_low, values, preferred_element_type=jnp.float32)
    attended_low = attended.astype(jnp.bfloat16).reshape(n_rows, width)
    projected = jnp.dot(attended_low, w_output, preferred_element_type=jnp.float32) + bias_output
    middle = rows_in + scale_one * projected
    second_low = layer_norm(middle, gain_two, shift_two).astype(jnp.bfloat16)
    hidden = jnp.dot(second_low, w_expand, preferred_element_type=jnp.float32) + bias_expand
    activated_low = jax.nn.gelu(hidden, approximate=False).astype(jnp.bfloat16)
    branch = jnp.dot(activated_low, w_reduce, preferred_element_type=jnp.float32) + bias_reduce
    outputs = middle + scale_two * branch
    back_input, back_output, back_expand, back_reduce = (w_input, w_output, w_expand, w_reduce)
    grad_out = cotangent.astype(jnp.float32).reshape(n_rows, width) * row_mask
    grad_branch = (grad_out * scale_two).astype(jnp.bfloat16)
    grad_scale_two = jnp.sum(grad_out * branch, axis=0)
    grad_bias_reduce = column_sum(grad_branch)
    grad_w_reduce = contract_rows(activated_low, grad_branch)
    grad_activated = contract_cols(grad_branch, back_reduce)
    gelu_exact = partial(jax.nn.gelu, approximate=False)
    _, gelu_back = jax.vjp(gelu_exact, hidden)
    grad_hidden = gelu_back(grad_activated)[0].astype(jnp.bfloat16)
    grad_bias_expand = column_sum(grad_hidden)
    grad_w_expand = contract_rows(second_low, grad_hidden)
    grad_second = contract_cols(grad_hidden, back_expand)
    _, norm_back_two = jax.vjp(layer_norm, middle, gain_two, shift_two)
    grad_middle, grad_gain_two, grad_shift_two = norm_back_two(grad_second)
    grad_middle = grad_middle + grad_out
    grad_projected = (grad_middle * scale_one).astype(jnp.bfloat16)
    grad_scale_one = jnp.sum(grad_middle * projected, axis=0)
    grad_bias_output = column_sum(grad_projected)
    grad_w_output = contract_rows(attended_low, grad_projected)
    grad_attended = (
        contract_cols(grad_projected, back_output).astype(jnp.bfloat16).reshape(head_shape)
    )
    scores = attention_scores()
    soft_full = jnp.exp(scores - log_total)
    soft_again = soft_full.astype(jnp.bfloat16)
    grad_soft = jnp.einsum(
        "iphd,iqhd->ihpq", grad_attended, values, preferred_element_type=jnp.float32
    )
    grad_values = jnp.einsum(
        "ihpq,iphd->iqhd", soft_again, grad_attended, preferred_element_type=jnp.float32
    ).astype(jnp.bfloat16)
    grad_scores = (
        soft_full * (grad_soft - jnp.sum(soft_full * grad_soft, axis=-1, keepdims=True))
    ).astype(jnp.bfloat16)
    grad_queries = (
        (
            jnp.einsum("ihpq,iqhd->iphd", grad_scores, key_rows, preferred_element_type=jnp.float32)
            * score_scale
        )
        .astype(jnp.bfloat16)
        .reshape(n_rows, width)
    )
    grad_keys = (
        (
            jnp.einsum("ihpq,iphd->iqhd", grad_scores, queries, preferred_element_type=jnp.float32)
            * score_scale
        )
        .astype(jnp.bfloat16)
        .reshape(n_rows, width)
    )
    grad_values = grad_values.reshape(n_rows, width)
    grad_bias_query = column_sum(grad_queries)
    grad_bias_value = column_sum(grad_values)
    grad_projections = jnp.concatenate([grad_queries, grad_keys, grad_values], axis=1)
    grad_w_input = contract_rows(normed_low, grad_projections)
    grad_normed = contract_cols(grad_projections, back_input)
    _, norm_back_one = jax.vjp(layer_norm, rows_in, gain_one, shift_one)
    grad_rows, grad_gain_one, grad_shift_one = norm_back_one(grad_normed)
    input_grad = grad_rows + grad_middle
    grads = (
        grad_gain_one,
        grad_shift_one,
        grad_bias_query,
        grad_bias_value,
        grad_bias_output,
        grad_scale_one,
        grad_gain_two,
        grad_shift_two,
        grad_bias_reduce,
        grad_scale_two,
    )
    side_grad = jnp.concatenate(
        [jnp.stack(grads, axis=1), grad_bias_expand.reshape(width, fold)], axis=1
    )
    side_grad = jnp.pad(side_grad, ((0, 0), (0, LANES - side_grad.shape[1])))
    low = jnp.bfloat16
    sum_reduce = scatter([grad_w_reduce.astype(low)], count)
    sum_second = scatter([grad_w_output.astype(low), grad_w_expand.astype(low)], count)
    sum_first = scatter([grad_w_input.astype(low), side_grad.astype(low)], count)
    sums = tuple(sum_first[:, columns + t] for t in range(len(grads)))
    sum_bias_expand = sum_first[:, columns + len(grads) : columns + len(grads) + fold].reshape(-1)
    return (
        outputs.reshape(n_images, n_patch, width).astype(jnp.bfloat16),
        input_grad.reshape(n_images, n_patch, width),
        sum_first[:, :columns],
        sum_second[:, :width],
        sum_second[:, width:],
        sum_reduce,
        *sums[:8],
        sum_bias_expand,
        *sums[8:],
    )


def solution(mesh):
    placed = (
        P(("wide", "narrow"), None, None),
        P(("wide", "narrow")),
        P(("wide", "narrow"), None, None),
        P(("wide", "narrow"), None),
        P(("wide", "narrow"), None),
        P(("wide", "narrow"), None),
        P(("wide", "narrow"), None),
        P(("wide", "narrow")),
        P(("wide", "narrow")),
        P(("wide", "narrow")),
        P(("wide", "narrow")),
        P(("wide", "narrow")),
        P(("wide", "narrow")),
        P(("wide", "narrow")),
        P(("wide", "narrow")),
        P(("wide", "narrow")),
        P(("wide", "narrow")),
        P(("wide", "narrow")),
    )
    return jax.shard_map(
        per_device,
        mesh=mesh,
        in_specs=placed,
        out_specs=(
            P(("wide", "narrow"), None, None),
            P(("wide", "narrow"), None, None),
            P(("wide", "narrow"), None),
            P(("wide", "narrow"), None),
            P(("wide", "narrow"), None),
            P(("wide", "narrow"), None),
            P(("wide", "narrow")),
            P(("wide", "narrow")),
            P(("wide", "narrow")),
            P(("wide", "narrow")),
            P(("wide", "narrow")),
            P(("wide", "narrow")),
            P(("wide", "narrow")),
            P(("wide", "narrow")),
            P(("wide", "narrow")),
            P(("wide", "narrow")),
            P(("wide", "narrow")),
        ),
        check_vma=False,
    )
```

```python
from functools import partial

import jax
import jax.numpy as jnp
from jax import lax
from jax.experimental import pallas as pl
from jax.experimental.pallas import tpu as pltpu
from jax.sharding import PartitionSpec as P


HEADS = 12
HEAD = 64
AXES = ("wide", "narrow")
LANES = 128
TAIL_RATE = 0.3
TAIL = (
    0.11962930113077164,
    0.12075396627187729,
    0.09991341084241867,
    0.12856192886829376,
    -0.05368424579501152,
    0.20635420083999634,
    -0.15720349550247192,
    0.03567487746477127,
)
BELL = 0.3989422804014327
PEAK = 1.1535e15


SCALARS = pl.BlockSpec(memory_space=pltpu.SMEM)


def shuffle(value, count, target):
    return lax.ppermute(value, AXES, [(d, target(d)) for d in range(count)])


def digits(planes):
    radices = []
    while planes > 1:
        radix = 4 if planes % 4 == 0 else 2 if planes % 2 == 0 else planes
        radices.append(radix)
        planes //= radix
    return radices


def shifted(device, stride, radix, step):
    digit = (device // stride) % radix
    return device + (((digit + step) % radix) - digit) * stride


def gather_z(shard, count):
    held = shard[None]
    stride = 8
    for radix in digits(count // 8):
        pieces = [held] + [
            shuffle(held, count, lambda d, s=s: shifted(d, stride, radix, s))
            for s in range(1, radix)
        ]
        held = jnp.concatenate(pieces, axis=0)
        stride *= radix
    return held


def plane_at(me, index, count):
    plane, stride, scale = 0, 1, 1
    place = lax.div(me, 8)
    for radix in digits(count // 8):
        step = lax.rem(lax.div(index, scale), radix)
        digit = lax.rem(lax.div(place, stride), radix)
        plane = plane + lax.rem(digit + radix - step, radix) * stride
        stride *= radix
        scale *= radix
    return plane


def gather_xy(own, count):
    half = own.shape[0] - own.shape[0] // 2
    across_x = shuffle(own, count, lambda d: d ^ 2)
    across_y = shuffle(own, count, lambda d: d ^ 4)
    far_y = shuffle(across_y[:half], count, lambda d: d ^ 2)
    pieces = [own, across_x, across_y, far_y]
    if half < own.shape[0]:
        pieces.append(shuffle(across_x[half:], count, lambda d: d ^ 4))
    return pieces


def spots(me):
    return lax.rem(me, 2), lax.rem(lax.div(me, 2), 2), lax.rem(lax.div(me, 4), 2)


def place_kernel(me_ref, *refs, half):
    out = refs[-1]
    each = (len(refs) - 1) // 2
    core, x, y = spots(me_ref[0])
    for side, pieces in ((core, refs[:each]), (1 - core, refs[each:-1])):
        out[0, 2 * y + x, side] = pieces[0][0]
        out[0, 2 * y + 1 - x, side] = pieces[1][0]
        out[0, 2 * (1 - y) + x, side] = pieces[2][0]
        far = pieces[3][0]
        if each > 4:
            far = jnp.where(pl.program_id(0) < half, far, pieces[4][0])
        out[0, 2 * (1 - y) + 1 - x, side] = far


def here():
    return lax.axis_index(AXES).astype(jnp.int32).reshape(1)


def assemble(pieces, count):
    twins = [shuffle(piece, count, lambda d: d ^ 1) for piece in pieces]
    rows, columns = pieces[0].shape[1:]
    planes, half = count // 8, pieces[3].shape[0]
    block = (1, rows, columns)
    every = pl.BlockSpec(block, lambda s, me: (s, 0, 0))
    near = pl.BlockSpec(block, lambda s, me: (jnp.minimum(s, half - 1), 0, 0))
    rest = pl.BlockSpec(block, lambda s, me: (jnp.maximum(s - half, 0), 0, 0))
    specs = ([every] * 3 + [near, rest])[: len(pieces)]
    full = pl.pallas_call(
        partial(place_kernel, half=half),
        grid_spec=pltpu.PrefetchScalarGridSpec(
            num_scalar_prefetch=1,
            grid=(planes,),
            in_specs=specs * 2,
            out_specs=pl.BlockSpec(
                (1, 4, 2, rows, columns), lambda s, me: (plane_at(me[0], s, count), 0, 0, 0, 0)
            ),
        ),
        out_shape=jax.ShapeDtypeStruct((planes, 4, 2, rows, columns), pieces[0].dtype),
        name="place",
    )(here(), *pieces, *twins)
    return full.reshape(count * rows, columns)


def take(value, index, axis):
    return lax.dynamic_index_in_dim(value, index, axis, keepdims=False)


def pack_kernel(me_ref, *refs):
    first = 0
    for part in refs[:-1]:
        refs[-1][0, :, :, first : first + part.shape[-1]] = part[0, :, 0]
        first += part.shape[-1]


def fold_kernel(me_ref, *refs, half):
    parts, (came, mine, to_x, to_y, far_x, far_y) = refs[:-6], refs[-6:]
    step = pl.program_id(0)
    _, x, y = spots(me_ref[0])

    def summed(spot):
        first = 0
        sums = []
        for part in parts:
            columns = slice(first, first + part.shape[-1])
            sums.append(
                part[0, spot, 0].astype(jnp.float32) + came[0, spot, :, columns].astype(jnp.float32)
            )
            first += part.shape[-1]
        return sums

    def put(ref, sums):
        first = 0
        for item in sums:
            ref[0, :, first : first + item.shape[-1]] = item.astype(ref.dtype)
            first += item.shape[-1]

    put(mine, summed(2 * y + x))
    put(to_x, summed(2 * y + 1 - x))
    put(to_y, summed(2 * (1 - y) + x))
    far = 2 * (1 - y) + 1 - x

    @pl.when(step < half)
    def _():
        put(far_x, summed(far))

    @pl.when(step >= half)
    def _():
        put(far_y, summed(far))


def merge_kernel(to_x, to_y, came_x, came_y, out_x, out_y):
    out_y[...] = (to_y[...].astype(jnp.float32) + came_x[...].astype(jnp.float32)).astype(out_y.dtype)
    out_x[...] = (to_x[...].astype(jnp.float32) + came_y[...].astype(jnp.float32)).astype(out_x.dtype)


def scatter_xy(parts, count):
    planes = count // 8
    half = planes // 2
    low, full = jnp.bfloat16, jnp.float32
    rows = parts[0].shape[0] // count
    columns = sum(p.shape[1] for p in parts)
    split = [p.reshape(planes, 4, 2, rows, p.shape[1]) for p in parts]
    me = here()
    shape = jax.ShapeDtypeStruct

    def of_core(flip):
        return [
            pl.BlockSpec(
                (1, 4, 1, rows, p.shape[1]),
                lambda s, me: (s, 0, lax.rem(me[0] + flip, 2), 0, 0),
            )
            for p in parts
        ]

    both = pl.BlockSpec((1, 4, rows, columns), lambda s, me: (s, 0, 0, 0))
    block = (1, rows, columns)
    every = pl.BlockSpec(block, lambda s, me: (s, 0, 0))
    send = pl.pallas_call(
        pack_kernel,
        grid_spec=pltpu.PrefetchScalarGridSpec(
            num_scalar_prefetch=1, grid=(planes,), in_specs=of_core(1), out_specs=both
        ),
        out_shape=shape((planes, 4, rows, columns), low),
        name="pack",
    )(me, *split)
    came = shuffle(send, count, lambda d: d ^ 1)
    mine, to_x, to_y, far_x, far_y = pl.pallas_call(
        partial(fold_kernel, half=half),
        grid_spec=pltpu.PrefetchScalarGridSpec(
            num_scalar_prefetch=1,
            grid=(planes,),
            in_specs=of_core(0) + [both],
            out_specs=[
                every,
                every,
                every,
                pl.BlockSpec(block, lambda s, me: (jnp.minimum(s, half - 1), 0, 0)),
                pl.BlockSpec(block, lambda s, me: (jnp.maximum(s - half, 0), 0, 0)),
            ],
        ),
        out_shape=[
            shape((planes, rows, columns), full),
            shape((planes, rows, columns), low),
            shape((planes, rows, columns), low),
            shape((half, rows, columns), low),
            shape((planes - half, rows, columns), low),
        ],
        name="fold",
    )(me, *split, came)
    came_x = shuffle(far_x, count, lambda d: d ^ 2)
    came_y = shuffle(far_y, count, lambda d: d ^ 4)
    lower = pl.BlockSpec(block, lambda s: (s, 0, 0))
    upper = pl.BlockSpec(block, lambda s: (s + half, 0, 0))
    to_x, to_y = pl.pallas_call(
        merge_kernel,
        grid=(half,),
        in_specs=[upper, lower, lower, lower],
        out_specs=[upper, lower],
        out_shape=[shape(to_x.shape, low), shape(to_y.shape, low)],
        input_output_aliases={0: 0, 1: 1},
        name="merge",
    )(to_x, to_y, came_x, came_y)
    from_x = shuffle(to_x, count, lambda d: d ^ 2)
    from_y = shuffle(to_y, count, lambda d: d ^ 4)
    return mine + from_x.astype(full) + from_y.astype(full)


def scatter_z(column, count):
    me = lax.axis_index(AXES)
    total = column
    stride = count
    for radix in digits(count // 8)[::-1]:
        stride //= radix
        mine = (me // stride) % radix
        split = total.reshape((radix, -1) + column.shape[1:])
        low = split.astype(jnp.bfloat16)
        total = take(split, mine, 0)
        for s in range(1, radix):
            item = take(low, (mine + s) % radix, 0)
            came = shuffle(item, count, lambda d, s=s: shifted(d, stride, radix, s))
            total = total + came.astype(jnp.float32)
    return total[0]


def scatter(parts, count):
    return scatter_z(scatter_xy(parts, count), count)


def after(value, other):
    return lax.optimization_barrier((value, other))[0]


def normalize(rows):
    centered = rows - jnp.mean(rows, axis=-1, keepdims=True)
    inverse = lax.rsqrt(jnp.mean(centered * centered, axis=-1, keepdims=True) + 1e-06)
    return centered * inverse, inverse


def dot_nn(left, right):
    return jnp.dot(left, right, preferred_element_type=jnp.float32)


def dot_nt(left, right):
    return lax.dot_general(
        left, right, (((1,), (1,)), ((), ())), preferred_element_type=jnp.float32
    )


def dot_tn(left, right):
    return lax.dot_general(
        left, right, (((0,), (0,)), ((), ())), preferred_element_type=jnp.float32
    )


def total(values):
    return jnp.sum(values, axis=0, keepdims=True)


def held(shape):
    return pl.BlockSpec(shape, lambda j: (0,) * len(shape), pipeline_mode=pl.Buffered(1))


def kept(shape):
    return pl.BlockSpec(shape, lambda j: (0,) * len(shape))


def chunk(shape, offset=0):
    return pl.BlockSpec(shape, lambda j: (0, j + offset))


def cost(flops, size=0):
    return pl.CostEstimate(flops=int(flops), transcendentals=0, bytes_accessed=int(size))


GAIN_ONE, SHIFT_ONE, BIAS_QUERY, BIAS_VALUE, BIAS_OUTPUT = 0, 1, 2, 3, 4
SCALE_ONE, GAIN_TWO, SHIFT_TWO, BIAS_REDUCE, SCALE_TWO = 5, 6, 7, 8, 9


def row(table, index):
    return table[index : index + 1, :]


def project_kernel(x_ref, side_ref, weight_ref, out_ref, table_ref, normed_ref):
    step = pl.program_id(0)

    @pl.when(step == 0)
    def _():
        table_ref[...] = side_ref[...].astype(jnp.float32).T[: table_ref.shape[0]]
        unit, _ = normalize(x_ref[...].astype(jnp.float32))
        normed = unit * row(table_ref, GAIN_ONE) + row(table_ref, SHIFT_ONE)
        normed_ref[...] = normed.astype(jnp.bfloat16)

    last = pl.num_programs(0) - 1
    bias = jnp.where(step == last, row(table_ref, BIAS_VALUE), jnp.zeros_like(row(table_ref, 0)))
    bias = jnp.where(step == 0, row(table_ref, BIAS_QUERY), bias)
    found = (dot_nn(normed_ref[...], weight_ref[...]) + bias).astype(jnp.bfloat16)
    scale = jnp.where(step == 0, HEAD**-0.5, 1.0).astype(jnp.bfloat16)
    out_ref[...] = found * scale


def project(x, first):
    rows, width = x.shape
    last = first.shape[1] // LANES - 1
    return pl.pallas_call(
        project_kernel,
        grid=(3,),
        in_specs=[
            held((rows, width)),
            pl.BlockSpec((width, LANES), lambda j: (0, last)),
            chunk((width, width)),
        ],
        out_specs=[chunk((rows, width)), kept((16, width))],
        out_shape=[
            jax.ShapeDtypeStruct((rows, 3 * width), jnp.bfloat16),
            jax.ShapeDtypeStruct((16, width), jnp.float32),
        ],
        scratch_shapes=[pltpu.VMEM((rows, width), jnp.bfloat16)],
        name="project",
        cost_estimate=cost(9e-6 * PEAK),
    )(x, first, first)


def halves(pair):
    lane = lax.broadcasted_iota(jnp.int32, pair.shape, 1)
    zero = jnp.zeros_like(pair)
    return jnp.where(lane < HEAD, pair, zero), jnp.where(lane < HEAD, zero, pair)


def join(left, right):
    lane = lax.broadcasted_iota(jnp.int32, left.shape, 1)
    return jnp.where(lane < HEAD, left, right)


def attend_kernel(counts_ref, q_ref, k_ref, v_ref, out_ref, lse_ref):
    patches = q_ref.shape[0]
    valid = lax.broadcasted_iota(jnp.int32, (patches, patches), 0) < counts_ref[pl.program_id(0)]
    for pair in range(HEADS // 2):
        lanes = slice(2 * HEAD * pair, 2 * HEAD * (pair + 1))
        q, k, v = q_ref[:, lanes], k_ref[:, lanes], v_ref[:, lanes]
        v_turned = v.astype(jnp.float32).T.astype(jnp.bfloat16)
        outs = []
        for side, k_half in enumerate(halves(k)):
            scores = jnp.where(valid, dot_nt(k_half, q), -1e30)
            top = jnp.max(scores, axis=0, keepdims=True)
            weights = jnp.exp(scores - top)
            mass = total(weights)
            lse_ref[2 * pair + side : 2 * pair + side + 1, :] = top + jnp.log(mass)
            mixed = dot_nn(v_turned[HEAD * side : HEAD * (side + 1)], weights.astype(jnp.bfloat16))
            outs.append(mixed / mass)
        out_ref[:, lanes] = jnp.concatenate(outs, axis=0).T.astype(jnp.bfloat16)


def attend(counts, qkv, patches):
    rows, width = qkv.shape[0], qkv.shape[1] // 3
    images = rows // patches
    part = lambda c: pl.BlockSpec((patches, width), lambda i: (i, c))
    return pl.pallas_call(
        attend_kernel,
        grid=(images,),
        in_specs=[SCALARS, part(0), part(1), part(2)],
        out_specs=[part(0), pl.BlockSpec((16, patches), lambda i: (i, 0))],
        out_shape=[
            jax.ShapeDtypeStruct((rows, width), jnp.bfloat16),
            jax.ShapeDtypeStruct((16 * images, patches), jnp.float32),
        ],
        name="attend",
        cost_estimate=cost(17e-6 * PEAK),
    )(counts, qkv, qkv, qkv)


def attend_back_kernel(counts_ref, q_ref, k_ref, v_ref, grad_ref, lse_ref, out_ref):
    patches, width = q_ref.shape
    valid = lax.broadcasted_iota(jnp.int32, (patches, patches), 0) < counts_ref[pl.program_id(0)]
    for pair in range(HEADS // 2):
        first = 2 * HEAD * pair
        lanes = slice(first, first + 2 * HEAD)
        q, k, v, grad = q_ref[:, lanes], k_ref[:, lanes], v_ref[:, lanes], grad_ref[:, lanes]
        k_turned = k.astype(jnp.float32).T.astype(jnp.bfloat16)
        grad_q, grad_k, grad_v = [], [], []
        for side, (k_half, v_half) in enumerate(zip(halves(k), halves(v))):
            lse = lse_ref[2 * pair + side : 2 * pair + side + 1, :]
            soft = jnp.where(valid, jnp.exp(dot_nt(k_half, q) - lse), 0.0)
            grad_soft = dot_nt(v_half, grad)
            inner = total(soft * grad_soft)
            grad_scores = (soft * (grad_soft - inner)).astype(jnp.bfloat16)
            grad_v.append(dot_nn(soft.astype(jnp.bfloat16), grad))
            grad_k.append(dot_nn(grad_scores, q))
            grad_q.append(dot_nn(k_turned[HEAD * side : HEAD * (side + 1)], grad_scores))
        whole_q = jnp.concatenate(grad_q, axis=0).T * HEAD**-0.5
        out_ref[:, lanes] = whole_q.astype(jnp.bfloat16)
        out_ref[:, width + first : width + first + 2 * HEAD] = join(*grad_k).astype(jnp.bfloat16)
        out_ref[:, 2 * width + first : 2 * width + first + 2 * HEAD] = join(*grad_v).astype(
            jnp.bfloat16
        )


def attend_back(counts, qkv, grad, lse, patches):
    rows, width = grad.shape
    part = lambda c: pl.BlockSpec((patches, width), lambda i: (i, c))
    return pl.pallas_call(
        attend_back_kernel,
        grid=(rows // patches,),
        in_specs=[
            SCALARS,
            part(0),
            part(1),
            part(2),
            part(0),
            pl.BlockSpec((16, patches), lambda i: (i, 0)),
        ],
        out_specs=pl.BlockSpec((patches, 3 * width), lambda i: (i, 0)),
        out_shape=jax.ShapeDtypeStruct((rows, 3 * width), jnp.bfloat16),
        name="attend_back",
        cost_estimate=cost(17e-6 * PEAK),
    )(counts, qkv, qkv, qkv, grad, lse)


def gelu_parts(u):
    bell = jnp.exp(-0.5 * (u * u))
    t = pl.reciprocal(1.0 + TAIL_RATE * jnp.abs(u))
    tail = TAIL[-1]
    for term in TAIL[-2::-1]:
        tail = tail * t + term
    tail = tail * t * bell
    below = jnp.where(u < 0.0, tail, 1.0 - tail)
    return u * below, below + u * bell * BELL


def blocks_of(rows, size):
    return [slice(size * i, size * (i + 1)) for i in range(rows // size)]


def masked(cot_ref, counts_ref, i, block):
    values = cot_ref[block, :].astype(jnp.float32)
    position = lax.broadcasted_iota(jnp.int32, values.shape, 0)
    return jnp.where(position < counts_ref[i], values, 0.0)


def expand_kernel(
    o_ref, x_ref, table_ref, bias_ref, w_output_ref, w_expand_ref,
    g_ref, slope_ref, mid_ref, turned_ref, normed_ref, *, size,
):
    low = jnp.bfloat16
    blocks = blocks_of(o_ref.shape[0], size)

    @pl.when(pl.program_id(0) == 0)
    def _():
        for block in blocks:
            a = dot_nn(o_ref[block, :], w_output_ref[...]) + row(table_ref, BIAS_OUTPUT)
            mid = x_ref[block, :].astype(jnp.float32) + row(table_ref, SCALE_ONE) * a
            mid_ref[block, :] = mid
            unit, _ = normalize(mid)
            normed = unit * row(table_ref, GAIN_TWO) + row(table_ref, SHIFT_TWO)
            normed_ref[block, :] = normed.astype(low)
            turned_ref[:, block] = normed.T.astype(low)

    for block in blocks:
        g, slope = gelu_parts(dot_nn(normed_ref[block, :], w_expand_ref[...]) + bias_ref[...])
        g_ref[block, :] = g.astype(low)
        slope_ref[block, :] = slope.astype(low)


def expand(o, x, table, bias, second, size):
    rows, width = o.shape
    hidden = bias.shape[1]
    low, shape = jnp.bfloat16, jax.ShapeDtypeStruct
    return pl.pallas_call(
        partial(expand_kernel, size=size),
        grid=(hidden // width,),
        in_specs=[
            held((rows, width)),
            held((rows, width)),
            held(table.shape),
            chunk((1, width)),
            held((width, width)),
            chunk((width, width), 1),
        ],
        out_specs=[
            chunk((rows, width)),
            chunk((rows, width)),
            kept((rows, width)),
            kept((width, rows)),
        ],
        out_shape=[
            shape((rows, hidden), low),
            shape((rows, hidden), low),
            shape((rows, width), jnp.float32),
            shape((width, rows), low),
        ],
        scratch_shapes=[pltpu.VMEM((rows, width), low)],
        name="expand",
        cost_estimate=cost(17e-6 * PEAK),
    )(o, x, table, bias, second, second)


def reduce_kernel(
    counts_ref, cot_ref, mid_ref, table_ref, g_ref, slope_ref, w_reduce_ref,
    act_ref, grad_u_ref, grad_w_reduce_ref, sums_ref, grad_bias_ref, grad_m_ref, m_ref,
):
    low = jnp.bfloat16
    rows, width = cot_ref.shape
    blocks = blocks_of(rows, rows // counts_ref.shape[0])
    step = pl.program_id(0)
    zero = jnp.zeros((1, width), jnp.float32)

    @pl.when(step == 0)
    def _():
        bias = zero
        for i, block in enumerate(blocks):
            grad_m = (row(table_ref, SCALE_TWO) * masked(cot_ref, counts_ref, i, block)).astype(low)
            grad_m_ref[block, :] = grad_m
            bias += total(grad_m.astype(jnp.float32))
            m_ref[block, :] = jnp.zeros((block.stop - block.start, width), jnp.float32)
        sums_ref[BIAS_REDUCE : BIAS_REDUCE + 1, :] = bias

    grad_bias = zero
    for block in blocks:
        grad_g = dot_nt(grad_m_ref[block, :], w_reduce_ref[...])
        grad_u = (grad_g * slope_ref[block, :].astype(jnp.float32)).astype(low)
        grad_u_ref[block, :] = grad_u
        grad_bias += total(grad_u.astype(jnp.float32))
        m_ref[block, :] += dot_nn(g_ref[block, :], w_reduce_ref[...])
    grad_bias_ref[...] = grad_bias
    grad_w_reduce_ref[...] = dot_tn(g_ref[...], grad_m_ref[...]).astype(low)

    @pl.when(step == pl.num_programs(0) - 1)
    def _():
        scale_two = zero
        for i, block in enumerate(blocks):
            m = m_ref[block, :] + row(table_ref, BIAS_REDUCE)
            act_ref[block, :] = (mid_ref[block, :] + row(table_ref, SCALE_TWO) * m).astype(low)
            scale_two += total(masked(cot_ref, counts_ref, i, block) * m)
        sums_ref[SCALE_TWO : SCALE_TWO + 1, :] = scale_two


def reduce(counts, cot, mid, table, g, slope, w_reduce):
    rows, width = cot.shape
    hidden = w_reduce.shape[0]
    low, full, shape = jnp.bfloat16, jnp.float32, jax.ShapeDtypeStruct
    down = pl.BlockSpec((width, width), lambda j: (j, 0))
    return pl.pallas_call(
        reduce_kernel,
        grid=(hidden // width,),
        in_specs=[
            SCALARS,
            held((rows, width)),
            held((rows, width)),
            held(table.shape),
            chunk((rows, width)),
            chunk((rows, width)),
            down,
        ],
        out_specs=[
            kept((rows, width)),
            chunk((rows, width)),
            down,
            kept(table.shape),
            chunk((1, width)),
        ],
        out_shape=[
            shape((rows, width), low),
            shape((rows, hidden), low),
            shape((hidden, width), low),
            shape(table.shape, full),
            shape((1, hidden), full),
        ],
        scratch_shapes=[pltpu.VMEM((rows, width), low), pltpu.VMEM((rows, width), full)],
        name="reduce",
        cost_estimate=cost(19e-6 * PEAK),
    )(counts, cot, mid, table, g, slope, w_reduce)


def norm_back(grad_normed, unit, inverse, gain):
    t = grad_normed * gain
    lean = jnp.mean(t, axis=-1, keepdims=True)
    tilt = jnp.mean(t * unit, axis=-1, keepdims=True)
    return (t - lean - unit * tilt) * inverse


def expand_back_kernel(
    counts_ref, o_ref, x_ref, cot_ref, mid_ref, turned_ref, table_ref, grad_u_ref,
    w_output_ref, w_expand_ref,
    grad_mid_ref, grad_o_ref, grad_w_output_ref, grad_w_expand_ref, sums_ref,
    grad_normed_ref, grad_a_ref,
):
    low = jnp.bfloat16
    rows, width = cot_ref.shape
    blocks = blocks_of(rows, rows // counts_ref.shape[0])
    step = pl.program_id(0)
    zero = jnp.zeros((1, width), jnp.float32)

    @pl.when(step == 0)
    def _():
        grad_normed_ref[...] = dot_nt(grad_u_ref[...], w_expand_ref[...])

    @pl.when(step > 0)
    def _():
        grad_normed_ref[...] += dot_nt(grad_u_ref[...], w_expand_ref[...])

    grad_w_expand_ref[...] = dot_nn(turned_ref[...], grad_u_ref[...]).astype(low)

    @pl.when(step == pl.num_programs(0) - 1)
    def _():
        gain_two, shift_two, scale_one, bias_output = zero, zero, zero, zero
        for i, block in enumerate(blocks):
            mid = mid_ref[block, :]
            unit, inverse = normalize(mid)
            grad_normed = grad_normed_ref[block, :]
            gain_two += total(grad_normed * unit)
            shift_two += total(grad_normed)
            grad_mid = masked(cot_ref, counts_ref, i, block) + norm_back(
                grad_normed, unit, inverse, row(table_ref, GAIN_TWO)
            )
            grad_mid_ref[block, :] = grad_mid
            scale_one += total(grad_mid * (mid - x_ref[block, :].astype(jnp.float32)))
            grad_a = (row(table_ref, SCALE_ONE) * grad_mid).astype(low)
            bias_output += total(grad_a.astype(jnp.float32))
            grad_a_ref[block, :] = grad_a
            grad_o_ref[block, :] = dot_nt(grad_a, w_output_ref[...]).astype(low)
        grad_w_output_ref[...] = dot_tn(o_ref[...], grad_a_ref[...]).astype(low)
        sums_ref[GAIN_TWO : GAIN_TWO + 1, :] = gain_two
        sums_ref[SHIFT_TWO : SHIFT_TWO + 1, :] = shift_two
        sums_ref[SCALE_ONE : SCALE_ONE + 1, :] = scale_one / row(table_ref, SCALE_ONE)
        sums_ref[BIAS_OUTPUT : BIAS_OUTPUT + 1, :] = bias_output


def expand_back(counts, o, x, cot, mid, turned, table, grad_u, second):
    rows, width = cot.shape
    hidden = grad_u.shape[1]
    low, full, shape = jnp.bfloat16, jnp.float32, jax.ShapeDtypeStruct
    return pl.pallas_call(
        expand_back_kernel,
        grid=(hidden // width,),
        in_specs=[
            SCALARS,
            held((rows, width)),
            held((rows, width)),
            held((rows, width)),
            held((rows, width)),
            held((width, rows)),
            held(table.shape),
            chunk((rows, width)),
            held((width, width)),
            chunk((width, width), 1),
        ],
        out_specs=[
            kept((rows, width)),
            kept((rows, width)),
            kept((width, width)),
            chunk((width, width)),
            kept(table.shape),
        ],
        out_shape=[
            shape((rows, width), full),
            shape((rows, width), low),
            shape((width, width), low),
            shape((width, hidden), low),
            shape(table.shape, full),
        ],
        scratch_shapes=[pltpu.VMEM((rows, width), full), pltpu.VMEM((rows, width), low)],
        name="expand_back",
        cost_estimate=cost(17e-6 * PEAK),
    )(counts, o, x, cot, mid, turned, table, grad_u, second, second)


def weigh_kernel(
    x_ref, side_ref, two_ref, back_ref, hidden_ref, grad_ref, weight_ref,
    grad_weight_ref, out_ref, turned_ref, rows_ref, gain_ref, shift_ref,
):
    step = pl.program_id(0)
    last = pl.num_programs(0) - 1

    @pl.when(step == 0)
    def _():
        for block in blocks_of(x_ref.shape[0], 256):
            unit, _ = normalize(x_ref[block, :].astype(jnp.float32))
            turned_ref[:, block] = unit.T.astype(jnp.bfloat16)
        rows_ref[...] = jnp.zeros(rows_ref.shape, jnp.float32)
        gain_ref[...] = jnp.zeros(gain_ref.shape, jnp.float32)
        shift_ref[...] = jnp.zeros(shift_ref.shape, jnp.float32)

    product = dot_nn(turned_ref[...], grad_ref[...])
    bias = total(grad_ref[...].astype(jnp.float32))
    weight = weight_ref[...].astype(jnp.float32)
    gain_ref[...] += jnp.sum(weight * product, axis=1, keepdims=True)
    shift_ref[...] += jnp.sum(weight * bias, axis=1, keepdims=True)
    gain = side_ref[:, GAIN_ONE : GAIN_ONE + 1].astype(jnp.float32)
    shift = side_ref[:, SHIFT_ONE : SHIFT_ONE + 1].astype(jnp.float32)
    grad_weight_ref[...] = (gain * product + shift * bias).astype(jnp.bfloat16)

    @pl.when(step == 0)
    def _():
        rows_ref[BIAS_QUERY : BIAS_QUERY + 1, :] = bias

    @pl.when(step == last)
    def _():
        rows_ref[BIAS_VALUE : BIAS_VALUE + 1, :] = bias
        rows_ref[BIAS_OUTPUT:BIAS_REDUCE, :] = back_ref[BIAS_OUTPUT:BIAS_REDUCE, :]
        rows_ref[BIAS_REDUCE : SCALE_TWO + 1, :] = two_ref[BIAS_REDUCE : SCALE_TWO + 1, :]
        rows_ref[SCALE_TWO + 1 : SCALE_TWO + 1 + hidden_ref.shape[0], :] = hidden_ref[...]
        turned = rows_ref[...].T
        lane = lax.broadcasted_iota(jnp.int32, turned.shape, 1)
        turned = jnp.where(lane == GAIN_ONE, gain_ref[...], turned)
        out_ref[...] = jnp.where(lane == SHIFT_ONE, shift_ref[...], turned).astype(jnp.bfloat16)


def weigh(x, two, back, hidden_rows, grad, first):
    rows, width = x.shape
    last = first.shape[1] // LANES - 1
    low, full, shape = jnp.bfloat16, jnp.float32, jax.ShapeDtypeStruct
    return pl.pallas_call(
        weigh_kernel,
        grid=(3,),
        in_specs=[
            held((rows, width)),
            pl.BlockSpec((width, LANES), lambda j: (0, last)),
            held(two.shape),
            held(back.shape),
            held(hidden_rows.shape),
            chunk((rows, width)),
            chunk((width, width)),
        ],
        out_specs=[chunk((width, width)), kept((width, LANES))],
        out_shape=[shape((width, 3 * width), low), shape((width, LANES), low)],
        scratch_shapes=[
            pltpu.VMEM((width, rows), low),
            pltpu.VMEM((LANES, width), full),
            pltpu.VMEM((width, 1), full),
            pltpu.VMEM((width, 1), full),
        ],
        name="weigh",
        cost_estimate=cost(9e-6 * PEAK),
    )(x, first, two, back, hidden_rows, grad, first)


def project_back_kernel(
    x_ref, table_ref, grad_ref, grad_mid_ref, weight_ref, grad_x_ref, grad_normed_ref
):
    step = pl.program_id(0)

    @pl.when(step == 0)
    def _():
        grad_normed_ref[...] = dot_nt(grad_ref[...], weight_ref[...])

    @pl.when(step > 0)
    def _():
        grad_normed_ref[...] += dot_nt(grad_ref[...], weight_ref[...])

    @pl.when(step == pl.num_programs(0) - 1)
    def _():
        for block in blocks_of(x_ref.shape[0], 256):
            unit, inverse = normalize(x_ref[block, :].astype(jnp.float32))
            grad_x_ref[block, :] = grad_mid_ref[block, :] + norm_back(
                grad_normed_ref[block, :], unit, inverse, row(table_ref, GAIN_ONE)
            )


def project_back(x, table, grad, grad_mid, first):
    rows, width = x.shape
    return pl.pallas_call(
        project_back_kernel,
        grid=(3,),
        in_specs=[
            held((rows, width)),
            held(table.shape),
            chunk((rows, width)),
            held((rows, width)),
            chunk((width, width)),
        ],
        out_specs=kept((rows, width)),
        out_shape=jax.ShapeDtypeStruct((rows, width), jnp.float32),
        scratch_shapes=[pltpu.VMEM((rows, width), jnp.float32)],
        name="project_back",
        cost_estimate=cost(10e-6 * PEAK),
    )(x, table, grad, grad_mid, first)


def join_kernel(*refs):
    vectors, hidden_ref, weight_ref, out_ref, rows_ref = refs[:-4], *refs[-4:]
    size, columns = weight_ref.shape
    rows_ref[...] = jnp.zeros(rows_ref.shape, jnp.float32)
    for t, ref in enumerate(vectors):
        rows_ref[t : t + 1, :] = ref[...].astype(jnp.float32)
    hidden = hidden_ref[...].astype(jnp.float32)
    for t in range(hidden.shape[1] // size):
        rows_ref[len(vectors) + t : len(vectors) + t + 1, :] = hidden[:, size * t : size * (t + 1)]
    out_ref[:, :columns] = weight_ref[...]
    out_ref[:, columns:] = rows_ref[...].T.astype(out_ref.dtype)


def join_side(vectors, hidden, weight):
    size, columns = weight.shape
    flat = [v.reshape(1, -1) for v in vectors + (hidden,)]
    return pl.pallas_call(
        join_kernel,
        out_shape=jax.ShapeDtypeStruct((size, columns + LANES), weight.dtype),
        scratch_shapes=[pltpu.VMEM((LANES, size), jnp.float32)],
        name="join_side",
    )(*flat, weight)


def layer(
    patches,
    counts,
    cotangent,
    input_weight,
    output_weight,
    expand_weight,
    reduce_weight,
    norm1_gain,
    norm1_shift,
    query_bias,
    value_bias,
    output_bias,
    branch1_scale,
    norm2_gain,
    norm2_shift,
    expand_bias,
    reduce_bias,
    branch2_scale,
):
    count = lax.axis_size("wide") * lax.axis_size("narrow")
    vectors = (
        norm1_gain,
        norm1_shift,
        query_bias,
        value_bias,
        output_bias,
        branch1_scale,
        norm2_gain,
        norm2_shift,
        reduce_bias,
        branch2_scale,
    )
    shard_rows = input_weight.shape[0]
    fold = expand_bias.shape[0] // shard_rows
    joined = join_side(vectors, expand_bias, input_weight)
    own_first = gather_z(joined, count)
    packed = jnp.concatenate([output_weight, expand_weight], axis=1)
    own_second = gather_z(after(packed, own_first), count)
    own_third = gather_z(after(reduce_weight, own_second), count)
    first = assemble(gather_xy(own_first, count), count)
    second = assemble(gather_xy(own_second, count), count)
    w_reduce = assemble(gather_xy(own_third, count), count)
    columns = input_weight.shape[1]
    n_images, n_patch, width = patches.shape
    n_rows = n_images * n_patch
    n_vectors = len(vectors)
    x = patches.reshape(n_rows, width)
    cot = cotangent.reshape(n_rows, width)
    qkv, table = project(x, first)
    hidden_rows = table[n_vectors : n_vectors + fold].reshape(fold, count, shard_rows)
    bias_expand = jnp.swapaxes(hidden_rows, 0, 1).reshape(1, -1)
    mixed, lse = attend(counts, qkv, n_patch)
    g, slope, mid, turned = expand(mixed, x, table, bias_expand, second, n_patch)
    activations, grad_u, grad_w_reduce, sums_two, grad_bias_expand = reduce(
        counts, cot, mid, table, g, slope, w_reduce
    )
    sum_reduce = scatter([grad_w_reduce], count)
    grad_mid, grad_mixed, grad_w_output, grad_w_expand, sums_back = expand_back(
        counts, mixed, x, cot, mid, turned, table, grad_u, second
    )
    sum_second = scatter([grad_w_output, grad_w_expand], count)
    grad_qkv = attend_back(counts, qkv, grad_mixed, lse, n_patch)
    grad_hidden = grad_bias_expand.reshape(count, fold, shard_rows)
    grad_hidden = jnp.swapaxes(grad_hidden, 0, 1).reshape(fold, width)
    grad_w_input, side_grad = weigh(x, sums_two, sums_back, grad_hidden, grad_qkv, first)
    input_grad = project_back(x, table, grad_qkv, grad_mid, first)
    sum_first = scatter([grad_w_input, side_grad], count)
    sums = sum_first[:, columns : columns + n_vectors + fold].T
    sum_bias_expand = sums[n_vectors:].reshape(-1)
    return (
        activations.reshape(n_images, n_patch, width),
        input_grad.reshape(n_images, n_patch, width),
        sum_first[:, :columns],
        sum_second[:, :width],
        sum_second[:, width:],
        sum_reduce,
        *sums[:8],
        sum_bias_expand,
        *sums[8:n_vectors],
    )


def solution(mesh):
    placed = (
        P(("wide", "narrow"), None, None),
        P(("wide", "narrow")),
        P(("wide", "narrow"), None, None),
        P(("wide", "narrow"), None),
        P(("wide", "narrow"), None),
        P(("wide", "narrow"), None),
        P(("wide", "narrow"), None),
        P(("wide", "narrow")),
        P(("wide", "narrow")),
        P(("wide", "narrow")),
        P(("wide", "narrow")),
        P(("wide", "narrow")),
        P(("wide", "narrow")),
        P(("wide", "narrow")),
        P(("wide", "narrow")),
        P(("wide", "narrow")),
        P(("wide", "narrow")),
        P(("wide", "narrow")),
    )
    return jax.shard_map(
        layer,
        mesh=mesh,
        in_specs=placed,
        out_specs=(
            P(("wide", "narrow"), None, None),
            P(("wide", "narrow"), None, None),
            P(("wide", "narrow"), None),
            P(("wide", "narrow"), None),
            P(("wide", "narrow"), None),
            P(("wide", "narrow"), None),
            P(("wide", "narrow")),
            P(("wide", "narrow")),
            P(("wide", "narrow")),
            P(("wide", "narrow")),
            P(("wide", "narrow")),
            P(("wide", "narrow")),
            P(("wide", "narrow")),
            P(("wide", "narrow")),
            P(("wide", "narrow")),
            P(("wide", "narrow")),
            P(("wide", "narrow")),
        ),
        check_vma=False,
    )
```

```python
from functools import partial

import jax
import jax.numpy as jnp
from jax import lax
from jax.experimental import pallas as pl
from jax.experimental.pallas import tpu as pltpu
from jax.sharding import PartitionSpec as P


HEADS = 12
HEAD = 64
AXES = ("wide", "narrow")
LANES = 128
TAIL_RATE = 0.3
TAIL = (
    0.11962930113077164,
    0.12075396627187729,
    0.09991341084241867,
    0.12856192886829376,
    -0.05368424579501152,
    0.20635420083999634,
    -0.15720349550247192,
    0.03567487746477127,
)
BELL = 0.3989422804014327
PEAK = 1.1535e15


SCALARS = pl.BlockSpec(memory_space=pltpu.SMEM)


def shuffle(value, count, target):
    return lax.ppermute(value, AXES, [(d, target(d)) for d in range(count)])


def digits(planes):
    radices = []
    while planes > 1:
        radix = 4 if planes % 4 == 0 else 2 if planes % 2 == 0 else planes
        radices.append(radix)
        planes //= radix
    return radices


def shifted(device, stride, radix, step):
    digit = (device // stride) % radix
    return device + (((digit + step) % radix) - digit) * stride


def gather_z(shard, count):
    held = shard[None]
    stride = 8
    for radix in digits(count // 8):
        pieces = [held] + [
            shuffle(held, count, lambda d, s=s: shifted(d, stride, radix, s))
            for s in range(1, radix)
        ]
        held = jnp.concatenate(pieces, axis=0)
        stride *= radix
    return held


def plane_at(me, index, count):
    plane, stride, scale = 0, 1, 1
    place = lax.div(me, 8)
    for radix in digits(count // 8):
        step = lax.rem(lax.div(index, scale), radix)
        digit = lax.rem(lax.div(place, stride), radix)
        plane = plane + lax.rem(digit + radix - step, radix) * stride
        stride *= radix
        scale *= radix
    return plane


def gather_xy(own, count):
    half = own.shape[0] - own.shape[0] // 2
    across_x = shuffle(own, count, lambda d: d ^ 2)
    across_y = shuffle(own, count, lambda d: d ^ 4)
    far_y = shuffle(across_y[:half], count, lambda d: d ^ 2)
    pieces = [own, across_x, across_y, far_y]
    if half < own.shape[0]:
        pieces.append(shuffle(across_x[half:], count, lambda d: d ^ 4))
    return pieces


def spots(me):
    return lax.rem(me, 2), lax.rem(lax.div(me, 2), 2), lax.rem(lax.div(me, 4), 2)


def place_kernel(me_ref, *refs, half):
    out = refs[-1]
    each = (len(refs) - 1) // 2
    core, x, y = spots(me_ref[0])
    for side, pieces in ((core, refs[:each]), (1 - core, refs[each:-1])):
        out[0, 2 * y + x, side] = pieces[0][0]
        out[0, 2 * y + 1 - x, side] = pieces[1][0]
        out[0, 2 * (1 - y) + x, side] = pieces[2][0]
        far = pieces[3][0]
        if each > 4:
            far = jnp.where(pl.program_id(0) < half, far, pieces[4][0])
        out[0, 2 * (1 - y) + 1 - x, side] = far


def here():
    return lax.axis_index(AXES).astype(jnp.int32).reshape(1)


def assemble(pieces, count):
    twins = [shuffle(piece, count, lambda d: d ^ 1) for piece in pieces]
    rows, columns = pieces[0].shape[1:]
    planes, half = count // 8, pieces[3].shape[0]
    block = (1, rows, columns)
    every = pl.BlockSpec(block, lambda s, me: (s, 0, 0))
    near = pl.BlockSpec(block, lambda s, me: (jnp.minimum(s, half - 1), 0, 0))
    rest = pl.BlockSpec(block, lambda s, me: (jnp.maximum(s - half, 0), 0, 0))
    specs = ([every] * 3 + [near, rest])[: len(pieces)]
    full = pl.pallas_call(
        partial(place_kernel, half=half),
        grid_spec=pltpu.PrefetchScalarGridSpec(
            num_scalar_prefetch=1,
            grid=(planes,),
            in_specs=specs * 2,
            out_specs=pl.BlockSpec(
                (1, 4, 2, rows, columns), lambda s, me: (plane_at(me[0], s, count), 0, 0, 0, 0)
            ),
        ),
        out_shape=jax.ShapeDtypeStruct((planes, 4, 2, rows, columns), pieces[0].dtype),
        name="place",
    )(here(), *pieces, *twins)
    return full.reshape(count * rows, columns)


def take(value, index, axis):
    return lax.dynamic_index_in_dim(value, index, axis, keepdims=False)


def pack_kernel(me_ref, *refs):
    first = 0
    for part in refs[:-1]:
        refs[-1][0, :, :, first : first + part.shape[-1]] = part[0, :, 0]
        first += part.shape[-1]


def fold_kernel(me_ref, *refs):
    parts, (came, mine, to_x, to_y, to_xy) = refs[:-5], refs[-5:]
    _, x, y = spots(me_ref[0])
    targets = (
        (mine, 2 * y + x),
        (to_x, 2 * y + 1 - x),
        (to_y, 2 * (1 - y) + x),
        (to_xy, 2 * (1 - y) + 1 - x),
    )
    for ref, spot in targets:
        first = 0
        for part in parts:
            columns = slice(first, first + part.shape[-1])
            kept = part[0, spot, 0] if len(part.shape) == 5 else part[0, spot]
            added = kept.astype(jnp.float32) + came[0, spot, :, columns].astype(jnp.float32)
            ref[0, :, columns] = added.astype(ref.dtype)
            first += part.shape[-1]


def split_rows(rows):
    return rows % 8 == 0


def put_split(send_ref, keep_ref, value, core):
    rows, columns = send_ref.shape[-2:]
    cut = value.reshape(-1, 2, rows, columns)
    even, odd = cut[:, 0], cut[:, 1]
    send = jnp.where(core == 0, odd, even).reshape(send_ref.shape)
    keep = jnp.where(core == 0, even, odd).reshape(keep_ref.shape)
    send_ref[...] = send.astype(send_ref.dtype)
    keep_ref[...] = keep.astype(keep_ref.dtype)


def pack(parts, count):
    planes = count // 8
    rows = parts[0].shape[0] // count
    columns = sum(p.shape[1] for p in parts)
    split = [p.reshape(planes, 4, 2, rows, p.shape[1]) for p in parts]
    send = pl.pallas_call(
        pack_kernel,
        grid_spec=pltpu.PrefetchScalarGridSpec(
            num_scalar_prefetch=1,
            grid=(planes,),
            in_specs=[of_core(p, 1) for p in split],
            out_specs=pl.BlockSpec((1, 4, rows, columns), lambda s, me: (s, 0, 0, 0)),
        ),
        out_shape=jax.ShapeDtypeStruct((planes, 4, rows, columns), jnp.bfloat16),
        name="pack",
    )(here(), *split)
    return send, split


def of_core(part, flip):
    if len(part.shape) == 4:
        return pl.BlockSpec((1,) + part.shape[1:], lambda s, me: (s, 0, 0, 0))
    return pl.BlockSpec(
        (1, 4, 1) + part.shape[3:], lambda s, me: (s, 0, lax.rem(me[0] + flip, 2), 0, 0)
    )


def scatter_xy(send, keep, count):
    planes, _, rows, columns = send.shape
    low, full = jnp.bfloat16, jnp.float32
    shape = jax.ShapeDtypeStruct
    every = pl.BlockSpec((1, rows, columns), lambda s, me: (s, 0, 0))
    came = shuffle(send, count, lambda d: d ^ 1)
    mine, *items = pl.pallas_call(
        fold_kernel,
        grid_spec=pltpu.PrefetchScalarGridSpec(
            num_scalar_prefetch=1,
            grid=(planes,),
            in_specs=[of_core(p, 0) for p in keep] + [of_core(came, 0)],
            out_specs=[every] * 4,
        ),
        out_shape=[shape((planes, rows, columns), full)]
        + [shape((planes, rows, columns), low)] * 3,
        name="fold",
    )(here(), *keep, came)
    for flip, item in zip((2, 4, 6), items):
        mine = mine + shuffle(item, count, lambda d: d ^ flip).astype(full)
    return mine


def scatter_z(column, count):
    me = lax.axis_index(AXES)
    total = column
    stride = count
    for radix in digits(count // 8)[::-1]:
        stride //= radix
        mine = (me // stride) % radix
        split = total.reshape((radix, -1) + column.shape[1:])
        low = split.astype(jnp.bfloat16)
        total = take(split, mine, 0)
        for s in range(1, radix):
            item = take(low, (mine + s) % radix, 0)
            came = shuffle(item, count, lambda d, s=s: shifted(d, stride, radix, s))
            total = total + came.astype(jnp.float32)
    return total[0]


def scatter(send, keep, count):
    return scatter_z(scatter_xy(send, keep, count), count)


def after(value, other):
    return lax.optimization_barrier((value, other))[0]


LOG2_E = 1.4426950408889634


def normalize(rows):
    centered = rows - jnp.mean(rows, axis=-1, keepdims=True)
    inverse = lax.rsqrt(jnp.mean(centered * centered, axis=-1, keepdims=True) + 1e-06)
    return centered * inverse, inverse


def dot_nn(left, right):
    return jnp.dot(left, right, preferred_element_type=jnp.float32)


def dot_nt(left, right):
    return lax.dot_general(
        left, right, (((1,), (1,)), ((), ())), preferred_element_type=jnp.float32
    )


def dot_tn(left, right):
    return lax.dot_general(
        left, right, (((0,), (0,)), ((), ())), preferred_element_type=jnp.float32
    )


def total(values):
    return jnp.sum(values, axis=0, keepdims=True)


def held(shape):
    return pl.BlockSpec(shape, lambda j: (0,) * len(shape), pipeline_mode=pl.Buffered(1))


def kept(shape):
    return pl.BlockSpec(shape, lambda j: (0,) * len(shape))


def chunk(shape, offset=0):
    return pl.BlockSpec(shape, lambda j: (0, j + offset))


def cost(flops, size=0):
    return pl.CostEstimate(flops=int(flops), transcendentals=0, bytes_accessed=int(size))


GAIN_ONE, SHIFT_ONE, BIAS_QUERY, BIAS_VALUE, BIAS_OUTPUT = 0, 1, 2, 3, 4
SCALE_ONE, GAIN_TWO, SHIFT_TWO, BIAS_REDUCE, SCALE_TWO = 5, 6, 7, 8, 9


def row(table, index):
    return table[index : index + 1, :]


def project_kernel(x_ref, first_ref, out_ref, table_ref):
    width = x_ref.shape[1]

    @pl.when(pl.program_id(0) == 0)
    def _():
        table_ref[...] = first_ref[:, 3 * width :].astype(jnp.float32).T[: table_ref.shape[0]]

    unit, _ = normalize(x_ref[...].astype(jnp.float32))
    normed = unit * row(table_ref, GAIN_ONE) + row(table_ref, SHIFT_ONE)
    normed = normed.astype(jnp.bfloat16)
    for part, bias in enumerate((BIAS_QUERY, None, BIAS_VALUE)):
        columns = slice(width * part, width * (part + 1))
        found = dot_nn(normed, first_ref[:, columns])
        if bias is not None:
            found = found + row(table_ref, bias)
        found = found.astype(jnp.bfloat16)
        if part == 0:
            found = found * jnp.bfloat16(HEAD**-0.5)
        out_ref[:, columns] = found


def across(size, width):
    return pl.BlockSpec((size, width), lambda i: (i, 0))


def project(x, first, size):
    rows, width = x.shape
    return pl.pallas_call(
        project_kernel,
        grid=(rows // size,),
        in_specs=[across(size, width), held(first.shape)],
        out_specs=[across(size, 3 * width), kept((16, width))],
        out_shape=[
            jax.ShapeDtypeStruct((rows, 3 * width), jnp.bfloat16),
            jax.ShapeDtypeStruct((16, width), jnp.float32),
        ],
        name="project",
        cost_estimate=cost(9e-6 * PEAK),
    )(x, first)


def halves(pair):
    lane = lax.broadcasted_iota(jnp.int32, pair.shape, 1)
    zero = jnp.zeros_like(pair)
    return jnp.where(lane < HEAD, pair, zero), jnp.where(lane < HEAD, zero, pair)


def join(left, right):
    lane = lax.broadcasted_iota(jnp.int32, left.shape, 1)
    return jnp.where(lane < HEAD, left, right)


def pair_lanes(pair):
    return slice(2 * HEAD * pair, 2 * HEAD * (pair + 1))


def attend_kernel(counts_ref, q_ref, k_ref, v_ref, out_ref, lse_ref):
    patches = q_ref.shape[0]
    valid = lax.broadcasted_iota(jnp.int32, (patches, patches), 0) < counts_ref[pl.program_id(0)]

    def scores_of(pair):
        lanes = pair_lanes(pair)
        q = q_ref[:, lanes]
        return [jnp.where(valid, dot_nt(k, q), -1e30) for k in halves(k_ref[:, lanes])]

    ahead = scores_of(0)
    for pair in range(HEADS // 2):
        scores = ahead
        if pair + 1 < HEADS // 2:
            ahead = scores_of(pair + 1)
        lanes = pair_lanes(pair)
        v_turned = v_ref[:, lanes].astype(jnp.float32).T.astype(jnp.bfloat16)
        tops = [jnp.max(s, axis=0, keepdims=True) for s in scores]
        weights = [jnp.exp(s - top) for s, top in zip(scores, tops)]
        masses = [total(w) for w in weights]
        outs = []
        for side in range(2):
            head = 2 * pair + side
            lse_ref[head : head + 1, :] = tops[side] + jnp.log(masses[side])
            mixed = dot_nn(
                v_turned[HEAD * side : HEAD * (side + 1)], weights[side].astype(jnp.bfloat16)
            )
            outs.append(mixed / masses[side])
        out_ref[:, lanes] = jnp.concatenate(outs, axis=0).T.astype(jnp.bfloat16)


def attend(counts, qkv, patches):
    rows, width = qkv.shape[0], qkv.shape[1] // 3
    images = rows // patches
    part = lambda c: pl.BlockSpec((patches, width), lambda i: (i, c))
    return pl.pallas_call(
        attend_kernel,
        grid=(images,),
        in_specs=[SCALARS, part(0), part(1), part(2)],
        out_specs=[part(0), pl.BlockSpec((16, patches), lambda i: (i, 0))],
        out_shape=[
            jax.ShapeDtypeStruct((rows, width), jnp.bfloat16),
            jax.ShapeDtypeStruct((16 * images, patches), jnp.float32),
        ],
        name="attend",
        cost_estimate=cost(10e-6 * PEAK),
    )(counts, qkv, qkv, qkv)


def attend_back_kernel(counts_ref, q_ref, k_ref, v_ref, grad_ref, lse_ref, out_ref):
    patches, width = q_ref.shape
    low = jnp.bfloat16
    valid = lax.broadcasted_iota(jnp.int32, (patches, patches), 0) < counts_ref[pl.program_id(0)]

    def products_of(pair):
        lanes = pair_lanes(pair)
        q, grad = q_ref[:, lanes], grad_ref[:, lanes]
        sides = zip(halves(k_ref[:, lanes]), halves(v_ref[:, lanes]))
        return [(dot_nt(k, q), dot_nt(v, grad)) for k, v in sides]

    ahead = products_of(0)
    for pair in range(HEADS // 2):
        products = ahead
        if pair + 1 < HEADS // 2:
            ahead = products_of(pair + 1)
        lanes = pair_lanes(pair)
        q, grad = q_ref[:, lanes], grad_ref[:, lanes]
        k_turned = k_ref[:, lanes].astype(jnp.float32).T.astype(low)
        soft, grad_scores = [], []
        for side, (scores, grad_soft) in enumerate(products):
            lse = lse_ref[2 * pair + side : 2 * pair + side + 1, :]
            soft.append(jnp.where(valid, jnp.exp(scores - lse), 0.0))
            inner = total(soft[side] * grad_soft)
            grad_scores.append((soft[side] * (grad_soft - inner)).astype(low))
        grad_v = [dot_nn(p.astype(low), grad) for p in soft]
        grad_k = [dot_nn(d, q) for d in grad_scores]
        grad_q = [
            dot_nn(k_turned[HEAD * side : HEAD * (side + 1)], d)
            for side, d in enumerate(grad_scores)
        ]
        whole_q = jnp.concatenate(grad_q, axis=0).T * HEAD**-0.5
        for part, value in enumerate((whole_q, join(*grad_k), join(*grad_v))):
            first = width * part + lanes.start
            out_ref[:, first : first + 2 * HEAD] = value.astype(low)


def attend_back(counts, qkv, grad, lse, patches):
    rows, width = grad.shape
    part = lambda c: pl.BlockSpec((patches, width), lambda i: (i, c))
    return pl.pallas_call(
        attend_back_kernel,
        grid=(rows // patches,),
        in_specs=[
            SCALARS,
            part(0),
            part(1),
            part(2),
            part(0),
            pl.BlockSpec((16, patches), lambda i: (i, 0)),
        ],
        out_specs=pl.BlockSpec((patches, 3 * width), lambda i: (i, 0)),
        out_shape=jax.ShapeDtypeStruct((rows, 3 * width), jnp.bfloat16),
        name="attend_back",
        cost_estimate=cost(12e-6 * PEAK),
    )(counts, qkv, qkv, qkv, grad, lse)


def gelu_parts(u):
    bell = jnp.exp2((-0.5 * LOG2_E) * (u * u))
    t = pl.reciprocal(1.0 + TAIL_RATE * jnp.abs(u))
    tail = TAIL[-1]
    for term in TAIL[-2::-1]:
        tail = tail * t + term
    tail = tail * t * bell
    below = jnp.where(u < 0.0, tail, 1.0 - tail)
    return u * below, below + u * bell * BELL


def blocks_of(rows, size):
    return [slice(size * i, size * (i + 1)) for i in range(rows // size)]


def masked(cot_ref, counts_ref, i, block):
    values = cot_ref[block, :].astype(jnp.float32)
    position = lax.broadcasted_iota(jnp.int32, values.shape, 0)
    return jnp.where(position < counts_ref[i], values, 0.0)


def settle_kernel(o_ref, x_ref, table_ref, w_output_ref, mid_ref, normed_ref, turned_ref):
    a = dot_nn(o_ref[...], w_output_ref[...]) + row(table_ref, BIAS_OUTPUT)
    mid = x_ref[...].astype(jnp.float32) + row(table_ref, SCALE_ONE) * a
    mid_ref[...] = mid
    unit, _ = normalize(mid)
    normed = unit * row(table_ref, GAIN_TWO) + row(table_ref, SHIFT_TWO)
    normed_ref[...] = normed.astype(jnp.bfloat16)
    turned_ref[...] = normed.T.astype(jnp.bfloat16)


def settle(o, x, table, second, size):
    rows, width = o.shape
    low, shape = jnp.bfloat16, jax.ShapeDtypeStruct
    block = across(size, width)
    return pl.pallas_call(
        settle_kernel,
        grid=(rows // size,),
        in_specs=[block, block, held(table.shape), held((width, width))],
        out_specs=[block, block, chunk((width, size))],
        out_shape=[
            shape((rows, width), jnp.float32),
            shape((rows, width), low),
            shape((width, rows), low),
        ],
        name="settle",
        cost_estimate=cost(5e-6 * PEAK),
    )(o, x, table, second)


def put_weight(refs, value, me_ref):
    if len(refs) == 2:
        put_split(*refs, value, lax.rem(me_ref[0], 2))
    else:
        refs[0][...] = value.astype(refs[0].dtype)


def mix_kernel(
    me_ref, counts_ref, cot_ref, mid_ref, normed_ref, table_ref, bias_ref, w_expand_ref,
    w_reduce_ref, act_ref, grad_u_ref, sums_ref, grad_bias_ref, *refs,
):
    *grad_w_refs, grad_m_ref, m_ref, g_ref = refs
    low = jnp.bfloat16
    rows, width = cot_ref.shape
    blocks = blocks_of(rows, rows // counts_ref.shape[0])
    step = pl.program_id(0)
    zero = jnp.zeros((1, width), jnp.float32)

    @pl.when(step == 0)
    def _():
        bias = zero
        for i, block in enumerate(blocks):
            grad_m = (row(table_ref, SCALE_TWO) * masked(cot_ref, counts_ref, i, block)).astype(low)
            grad_m_ref[block, :] = grad_m
            bias += total(grad_m.astype(jnp.float32))
            m_ref[block, :] = jnp.zeros((block.stop - block.start, width), jnp.float32)
        sums_ref[BIAS_REDUCE : BIAS_REDUCE + 1, :] = bias

    grad_bias = zero
    for block in blocks:
        u = dot_nn(normed_ref[block, :], w_expand_ref[...]) + bias_ref[...]
        grad_g = dot_nt(grad_m_ref[block, :], w_reduce_ref[...])
        g, slope = gelu_parts(u)
        g = g.astype(low)
        g_ref[block, :] = g
        grad_u = (grad_g * slope).astype(low)
        grad_u_ref[block, :] = grad_u
        grad_bias += total(grad_u.astype(jnp.float32))
        m_ref[block, :] += dot_nn(g, w_reduce_ref[...])
    grad_bias_ref[...] = grad_bias
    put_weight(grad_w_refs, dot_tn(g_ref[...], grad_m_ref[...]), me_ref)

    @pl.when(step == pl.num_programs(0) - 1)
    def _():
        scale_two = zero
        for i, block in enumerate(blocks):
            m = m_ref[block, :] + row(table_ref, BIAS_REDUCE)
            act_ref[block, :] = (mid_ref[block, :] + row(table_ref, SCALE_TWO) * m).astype(low)
            scale_two += total(masked(cot_ref, counts_ref, i, block) * m)
        sums_ref[SCALE_TWO : SCALE_TWO + 1, :] = scale_two


def mix(counts, cot, mid, normed, table, bias, second, w_reduce, count):
    rows, width = cot.shape
    hidden = w_reduce.shape[0]
    low, full, shape = jnp.bfloat16, jnp.float32, jax.ShapeDtypeStruct
    down = pl.BlockSpec((width, width), lambda j: (j, 0))
    piece = hidden // count
    if split_rows(piece) and 8 * piece == width:
        halved = shape((count // 8, 4, piece, width), low)
        weights = [halved, halved]
        specs = [pl.BlockSpec((1, 4, piece, width), lambda j: (j, 0, 0, 0))] * 2
    else:
        weights, specs = [shape((hidden, width), low)], [down]
    results = pl.pallas_call(
        mix_kernel,
        grid=(hidden // width,),
        in_specs=[
            SCALARS,
            SCALARS,
            held((rows, width)),
            held((rows, width)),
            held((rows, width)),
            held(table.shape),
            chunk((1, width)),
            chunk((width, width), 1),
            down,
        ],
        out_specs=[
            kept((rows, width)),
            chunk((rows, width)),
            kept(table.shape),
            chunk((1, width)),
        ]
        + specs,
        out_shape=[
            shape((rows, width), low),
            shape((rows, hidden), low),
            shape(table.shape, full),
            shape((1, hidden), full),
        ]
        + weights,
        scratch_shapes=[
            pltpu.VMEM((rows, width), low),
            pltpu.VMEM((rows, width), full),
            pltpu.VMEM((rows, width), low),
        ],
        name="mix",
        cost_estimate=cost(36e-6 * PEAK),
    )(here(), counts, cot, mid, normed, table, bias, second, w_reduce)
    grads = results[4:]
    return results[:4], (grads[0], [grads[1]]) if len(grads) == 2 else pack(grads, count)


def norm_back(grad_normed, unit, inverse, gain):
    t = grad_normed * gain
    lean = jnp.mean(t, axis=-1, keepdims=True)
    tilt = jnp.mean(t * unit, axis=-1, keepdims=True)
    return (t - lean - unit * tilt) * inverse


def settle_back_kernel(
    counts_ref, x_ref, cot_ref, mid_ref, table_ref, grad_u_ref, second_ref,
    grad_mid_ref, grad_a_ref, grad_o_ref, sums_ref,
):
    low = jnp.bfloat16
    step = pl.program_id(0)
    width = x_ref.shape[1]
    grad_normed = dot_nt(grad_u_ref[...], second_ref[:, width:])
    mid = mid_ref[...]
    unit, inverse = normalize(mid)
    grad_y = masked(cot_ref, counts_ref, step, slice(None))
    grad_mid = grad_y + norm_back(grad_normed, unit, inverse, row(table_ref, GAIN_TWO))
    grad_mid_ref[...] = grad_mid
    grad_a = (row(table_ref, SCALE_ONE) * grad_mid).astype(low)
    grad_a_ref[...] = grad_a
    grad_o_ref[...] = dot_nt(grad_a, second_ref[:, :width]).astype(low)

    @pl.when(step == 0)
    def _():
        sums_ref[...] = jnp.zeros(sums_ref.shape, jnp.float32)

    sums_ref[GAIN_TWO : GAIN_TWO + 1, :] += total(grad_normed * unit)
    sums_ref[SHIFT_TWO : SHIFT_TWO + 1, :] += total(grad_normed)
    leaned = total(grad_mid * (mid - x_ref[...].astype(jnp.float32)))
    sums_ref[SCALE_ONE : SCALE_ONE + 1, :] += leaned / row(table_ref, SCALE_ONE)
    sums_ref[BIAS_OUTPUT : BIAS_OUTPUT + 1, :] += total(grad_a.astype(jnp.float32))


def settle_back(counts, x, cot, mid, table, grad_u, second):
    rows, width = cot.shape
    size = rows // counts.shape[0]
    low, full, shape = jnp.bfloat16, jnp.float32, jax.ShapeDtypeStruct
    block = across(size, width)
    return pl.pallas_call(
        settle_back_kernel,
        grid=(rows // size,),
        in_specs=[
            SCALARS,
            block,
            block,
            block,
            held(table.shape),
            across(size, grad_u.shape[1]),
            held(second.shape),
        ],
        out_specs=[block, block, block, kept(table.shape)],
        out_shape=[
            shape((rows, width), full),
            shape((rows, width), low),
            shape((rows, width), low),
            shape(table.shape, full),
        ],
        name="settle_back",
        cost_estimate=cost(12e-6 * PEAK),
    )(counts, x, cot, mid, table, grad_u, second)


def weigh_second_kernel(me_ref, o_ref, grad_a_ref, turned_ref, grad_u_ref, *refs):
    step = pl.program_id(0)

    @pl.when(step == 0)
    def _():
        put_weight(refs, dot_tn(o_ref[...], grad_a_ref[...]), me_ref)

    @pl.when(step > 0)
    def _():
        put_weight(refs, dot_nn(turned_ref[...], grad_u_ref[...]), me_ref)


def weigh_second(o, grad_a, turned, grad_u, count):
    rows, width = o.shape
    steps = 1 + grad_u.shape[1] // width
    low, shape = jnp.bfloat16, jax.ShapeDtypeStruct
    piece = width // count
    if split_rows(piece):
        weights = [shape((count // 8, 4, piece, steps * width), low)] * 2
        specs = [pl.BlockSpec((count // 8, 4, piece, width), lambda j: (0, 0, 0, j))] * 2
    else:
        weights, specs = [shape((width, steps * width), low)], [chunk((width, width))]
    grads = pl.pallas_call(
        weigh_second_kernel,
        grid=(steps,),
        in_specs=[
            SCALARS,
            held((rows, width)),
            held((rows, width)),
            held((width, rows)),
            pl.BlockSpec((rows, width), lambda j: (0, jnp.maximum(j - 1, 0))),
        ],
        out_specs=specs,
        out_shape=weights,
        name="weigh_second",
        cost_estimate=cost(12e-6 * PEAK),
    )(here(), o, grad_a, turned, grad_u)
    return (grads[0], [grads[1]]) if len(grads) == 2 else pack(grads, count)


def turn_kernel(row_ref, out_ref, rows_ref, *, size):
    fold, width = out_ref.shape
    count = width // size
    for d in range(count):
        rows_ref[d : d + 1, :] = row_ref[:, fold * size * d : fold * size * (d + 1)]
    lane = lax.broadcasted_iota(jnp.int32, (count, width), 1)
    mine = lax.div(lane, size) == lax.broadcasted_iota(jnp.int32, (count, width), 0)
    spread = lax.rem(lax.broadcasted_iota(jnp.int32, (size, width), 1), size)
    spread = spread == lax.broadcasted_iota(jnp.int32, (size, width), 0)
    spread = jnp.where(spread, 1.0, 0.0).astype(jnp.bfloat16)
    for j in range(fold):
        piece = rows_ref[:, size * j : size * (j + 1)].astype(jnp.bfloat16)
        out_ref[j : j + 1, :] = total(jnp.where(mine, dot_nn(piece, spread), 0.0))


def turn(row_values, fold, size):
    width = row_values.shape[1] // fold
    return pl.pallas_call(
        partial(turn_kernel, size=size),
        out_shape=jax.ShapeDtypeStruct((fold, width), jnp.float32),
        scratch_shapes=[pltpu.VMEM((width // size, fold * size), jnp.float32)],
        name="turn",
        cost_estimate=cost(3e-6 * PEAK),
    )(row_values)


def weigh_kernel(
    x_ref, side_ref, two_ref, back_ref, hidden_ref, grad_ref, weight_ref,
    grad_weight_ref, out_ref, turned_ref, rows_ref, gain_ref, shift_ref,
):
    step = pl.program_id(0)
    last = pl.num_programs(0) - 1

    @pl.when(step == 0)
    def _():
        for block in blocks_of(x_ref.shape[0], 256):
            unit, _ = normalize(x_ref[block, :].astype(jnp.float32))
            turned_ref[:, block] = unit.T.astype(jnp.bfloat16)
        rows_ref[...] = jnp.zeros(rows_ref.shape, jnp.float32)
        gain_ref[...] = jnp.zeros(gain_ref.shape, jnp.float32)
        shift_ref[...] = jnp.zeros(shift_ref.shape, jnp.float32)

    product = dot_nn(turned_ref[...], grad_ref[...])
    bias = total(grad_ref[...].astype(jnp.float32))
    weight = weight_ref[...].astype(jnp.float32)
    gain_ref[...] += jnp.sum(weight * product, axis=1, keepdims=True)
    shift_ref[...] += jnp.sum(weight * bias, axis=1, keepdims=True)
    gain = side_ref[:, GAIN_ONE : GAIN_ONE + 1].astype(jnp.float32)
    shift = side_ref[:, SHIFT_ONE : SHIFT_ONE + 1].astype(jnp.float32)
    grad_weight_ref[...] = (gain * product + shift * bias).astype(jnp.bfloat16)

    @pl.when(step == 0)
    def _():
        rows_ref[BIAS_QUERY : BIAS_QUERY + 1, :] = bias

    @pl.when(step == last)
    def _():
        rows_ref[BIAS_VALUE : BIAS_VALUE + 1, :] = bias
        rows_ref[BIAS_OUTPUT:BIAS_REDUCE, :] = back_ref[BIAS_OUTPUT:BIAS_REDUCE, :]
        rows_ref[BIAS_REDUCE : SCALE_TWO + 1, :] = two_ref[BIAS_REDUCE : SCALE_TWO + 1, :]
        rows_ref[SCALE_TWO + 1 : SCALE_TWO + 1 + hidden_ref.shape[0], :] = hidden_ref[...]
        turned = rows_ref[...].T
        lane = lax.broadcasted_iota(jnp.int32, turned.shape, 1)
        turned = jnp.where(lane == GAIN_ONE, gain_ref[...], turned)
        out_ref[...] = jnp.where(lane == SHIFT_ONE, shift_ref[...], turned).astype(jnp.bfloat16)


def weigh(x, two, back, hidden_rows, grad, first):
    rows, width = x.shape
    last = first.shape[1] // LANES - 1
    low, full, shape = jnp.bfloat16, jnp.float32, jax.ShapeDtypeStruct
    return pl.pallas_call(
        weigh_kernel,
        grid=(3,),
        in_specs=[
            held((rows, width)),
            pl.BlockSpec((width, LANES), lambda j: (0, last)),
            held(two.shape),
            held(back.shape),
            held(hidden_rows.shape),
            chunk((rows, width)),
            chunk((width, width)),
        ],
        out_specs=[chunk((width, width)), kept((width, LANES))],
        out_shape=[shape((width, 3 * width), low), shape((width, LANES), low)],
        scratch_shapes=[
            pltpu.VMEM((width, rows), low),
            pltpu.VMEM((LANES, width), full),
            pltpu.VMEM((width, 1), full),
            pltpu.VMEM((width, 1), full),
        ],
        name="weigh",
        cost_estimate=cost(9e-6 * PEAK),
    )(x, first, two, back, hidden_rows, grad, first)


def unturn_kernel(table_ref, out_ref, *, first, fold, size):
    width = table_ref.shape[1]
    count = width // size
    low = jnp.bfloat16
    lane = lax.broadcasted_iota(jnp.int32, (count, width), 1)
    mine = lax.div(lane, size) == lax.broadcasted_iota(jnp.int32, (count, width), 0)
    place = lax.rem(lax.broadcasted_iota(jnp.int32, (width, fold * size), 0), size)
    target = lax.broadcasted_iota(jnp.int32, (width, fold * size), 1)
    by_device = jnp.zeros((count, fold * size), jnp.float32)
    for j in range(fold):
        spread = jnp.where(mine, row(table_ref, first + j), 0.0).astype(low)
        choose = jnp.where(place + size * j == target, 1.0, 0.0).astype(low)
        by_device += dot_nn(spread, choose)
    whole = out_ref.shape[1]
    lane = lax.broadcasted_iota(jnp.int32, (fold * size, whole), 1)
    repeat = lax.rem(lane, fold * size) == lax.broadcasted_iota(jnp.int32, (fold * size, whole), 0)
    spread = dot_nn(by_device.astype(low), jnp.where(repeat, 1.0, 0.0).astype(low))
    lane = lax.broadcasted_iota(jnp.int32, (count, whole), 1)
    mine = lax.div(lane, fold * size) == lax.broadcasted_iota(jnp.int32, (count, whole), 0)
    out_ref[...] = total(jnp.where(mine, spread, 0.0))


def unturn(table, first, fold, size):
    return pl.pallas_call(
        partial(unturn_kernel, first=first, fold=fold, size=size),
        out_shape=jax.ShapeDtypeStruct((1, fold * table.shape[1]), jnp.float32),
        name="unturn",
        cost_estimate=cost(3e-6 * PEAK),
    )(table)


def project_back_kernel(x_ref, table_ref, grad_ref, grad_mid_ref, first_ref, grad_x_ref):
    grad_normed = dot_nt(grad_ref[...], first_ref[:, : grad_ref.shape[1]])
    unit, inverse = normalize(x_ref[...].astype(jnp.float32))
    grad_x_ref[...] = grad_mid_ref[...] + norm_back(
        grad_normed, unit, inverse, row(table_ref, GAIN_ONE)
    )


def project_back(x, table, grad, grad_mid, first, size):
    rows, width = x.shape
    block = across(size, width)
    return pl.pallas_call(
        project_back_kernel,
        grid=(rows // size,),
        in_specs=[
            block, held(table.shape), across(size, 3 * width), block, held(first.shape),
        ],
        out_specs=block,
        out_shape=jax.ShapeDtypeStruct((rows, width), jnp.float32),
        name="project_back",
        cost_estimate=cost(10e-6 * PEAK),
    )(x, table, grad, grad_mid, first)


def join_kernel(*refs):
    vectors, hidden_ref, weight_ref, out_ref, rows_ref = refs[:-4], *refs[-4:]
    size, columns = weight_ref.shape
    rows_ref[...] = jnp.zeros(rows_ref.shape, jnp.float32)
    for t, ref in enumerate(vectors):
        rows_ref[t : t + 1, :] = ref[...].astype(jnp.float32)
    hidden = hidden_ref[...].astype(jnp.float32)
    for t in range(hidden.shape[1] // size):
        rows_ref[len(vectors) + t : len(vectors) + t + 1, :] = hidden[:, size * t : size * (t + 1)]
    out_ref[:, :columns] = weight_ref[...]
    out_ref[:, columns:] = rows_ref[...].T.astype(out_ref.dtype)


def join_side(vectors, hidden, weight):
    size, columns = weight.shape
    flat = [v.reshape(1, -1) for v in vectors + (hidden,)]
    return pl.pallas_call(
        join_kernel,
        out_shape=jax.ShapeDtypeStruct((size, columns + LANES), weight.dtype),
        scratch_shapes=[pltpu.VMEM((LANES, size), jnp.float32)],
        name="join_side",
    )(*flat, weight)


def layer(
    patches,
    counts,
    cotangent,
    input_weight,
    output_weight,
    expand_weight,
    reduce_weight,
    norm1_gain,
    norm1_shift,
    query_bias,
    value_bias,
    output_bias,
    branch1_scale,
    norm2_gain,
    norm2_shift,
    expand_bias,
    reduce_bias,
    branch2_scale,
):
    count = lax.axis_size("wide") * lax.axis_size("narrow")
    vectors = (
        norm1_gain,
        norm1_shift,
        query_bias,
        value_bias,
        output_bias,
        branch1_scale,
        norm2_gain,
        norm2_shift,
        reduce_bias,
        branch2_scale,
    )
    shard_rows = input_weight.shape[0]
    fold = expand_bias.shape[0] // shard_rows
    joined = join_side(vectors, expand_bias, input_weight)
    own_first = gather_z(joined, count)
    packed = jnp.concatenate([output_weight, expand_weight], axis=1)
    own_second = gather_z(after(packed, own_first), count)
    own_third = gather_z(after(reduce_weight, own_second), count)
    first = assemble(gather_xy(own_first, count), count)
    second = assemble(gather_xy(own_second, count), count)
    w_reduce = assemble(gather_xy(own_third, count), count)
    columns = input_weight.shape[1]
    n_images, n_patch, width = patches.shape
    n_rows = n_images * n_patch
    n_vectors = len(vectors)
    x = patches.reshape(n_rows, width)
    cot = cotangent.reshape(n_rows, width)
    qkv, table = project(x, first, n_patch)
    bias_expand = unturn(table, n_vectors, fold, shard_rows)
    mixed, lse = attend(counts, qkv, n_patch)
    mid, normed, turned = settle(mixed, x, table, second, n_patch)
    (activations, grad_u, sums_two, grad_bias_expand), grad_w_reduce = mix(
        counts, cot, mid, normed, table, bias_expand, second, w_reduce, count
    )
    sum_reduce = scatter(*grad_w_reduce, count)
    grad_hidden = turn(grad_bias_expand, fold, shard_rows)
    grad_mid, grad_a, grad_mixed, sums_back = settle_back(
        counts, x, cot, mid, table, grad_u, second
    )
    grad_w_second = weigh_second(mixed, grad_a, turned, grad_u, count)
    sum_second = scatter(*grad_w_second, count)
    grad_qkv = attend_back(counts, qkv, grad_mixed, lse, n_patch)
    grad_w_input, side_grad = weigh(x, sums_two, sums_back, grad_hidden, grad_qkv, first)
    input_grad = project_back(x, table, grad_qkv, grad_mid, first, n_patch)
    sum_first = scatter(*pack([grad_w_input, side_grad], count), count)
    sums = sum_first[:, columns : columns + n_vectors + fold].T
    sum_bias_expand = sums[n_vectors:].reshape(-1)
    return (
        activations.reshape(n_images, n_patch, width),
        input_grad.reshape(n_images, n_patch, width),
        sum_first[:, :columns],
        sum_second[:, :width],
        sum_second[:, width:],
        sum_reduce,
        *sums[:8],
        sum_bias_expand,
        *sums[8:n_vectors],
    )


def solution(mesh):
    placed = (
        P(("wide", "narrow"), None, None),
        P(("wide", "narrow")),
        P(("wide", "narrow"), None, None),
        P(("wide", "narrow"), None),
        P(("wide", "narrow"), None),
        P(("wide", "narrow"), None),
        P(("wide", "narrow"), None),
        P(("wide", "narrow")),
        P(("wide", "narrow")),
        P(("wide", "narrow")),
        P(("wide", "narrow")),
        P(("wide", "narrow")),
        P(("wide", "narrow")),
        P(("wide", "narrow")),
        P(("wide", "narrow")),
        P(("wide", "narrow")),
        P(("wide", "narrow")),
        P(("wide", "narrow")),
    )
    return jax.shard_map(
        layer,
        mesh=mesh,
        in_specs=placed,
        out_specs=(
            P(("wide", "narrow"), None, None),
            P(("wide", "narrow"), None, None),
            P(("wide", "narrow"), None),
            P(("wide", "narrow"), None),
            P(("wide", "narrow"), None),
            P(("wide", "narrow"), None),
            P(("wide", "narrow")),
            P(("wide", "narrow")),
            P(("wide", "narrow")),
            P(("wide", "narrow")),
            P(("wide", "narrow")),
            P(("wide", "narrow")),
            P(("wide", "narrow")),
            P(("wide", "narrow")),
            P(("wide", "narrow")),
            P(("wide", "narrow")),
            P(("wide", "narrow")),
        ),
        check_vma=False,
    )
```
